256 devices in a mesh: ctx: 8 (over y, core), vocab: 32 (over x, z).
Axes of the slice: x: 4, y: 4, z: 8, core: 2. Of those that a mesh axis runs over, the one named last changes fastest.
Arguments:
- resid_out: bfloat16 [2048, 4096], P('ctx', 'vocab'), may hold values from -4 to 4
- final_gain: float32 [4096], replicated, may hold values from 0.5 to 1.5
- head_weight: bfloat16 [4096, 32768], P('ctx', 'vocab'), may hold values from -2 to 2
- targets: int32 [2048], P('ctx'), may hold values from 0 to 32767
- out_weight: bfloat16 [8192, 4096], P('vocab', 'ctx'), may hold values from -0.0625 to 0.0625
- norm_gain: float32 [8192], P('vocab'), may hold values from 0.5 to 1.5
- xs: bfloat16 [2048, 8192], P('ctx', 'vocab'), may hold values from -6 to 6
- gate_z: bfloat16 [2048, 8192], P('ctx', 'vocab'), may hold values from -6 to 6
- b_proj: bfloat16 [2048, 1024], P('ctx'), may hold values from -1.796875 to 1.796875
- c_proj: bfloat16 [2048, 1024], P('ctx'), may hold values from -1.796875 to 1.796875
- step_dt: float32 [128, 2048], P('vocab', 'ctx'), may hold values from 0.01 to 0.05
- log_decay: float32 [128, 2048], P('vocab', 'ctx'), may hold values from -2 to 0
- skip_d: float32 [128], P('vocab'), may hold values from 0.5 to 1.5
Outputs:
- grad_head: bfloat16 [4096, 32768], P('ctx', 'vocab')
- grad_resid: bfloat16 [2048, 4096], P('ctx', 'vocab')
- grad_out_weight: bfloat16 [8192, 4096], P('vocab', 'ctx')
- grad_xs: bfloat16 [2048, 8192], P('ctx', 'vocab')
- grad_gate: bfloat16 [2048, 8192], P('ctx', 'vocab')
- grad_b: bfloat16 [2048, 1024], P(('ctx', 'vocab'))
- grad_c: bfloat16 [2048, 1024], P(('ctx', 'vocab'))
- grad_dt: float32 [128, 2048], P('vocab', 'ctx')
- grad_log_decay: float32 [128, 2048], P('vocab', 'ctx')
The draws below stay inside these ranges and needn't reach their ends.
All inputs are finite; a program needn't handle non-finite values.
Results may differ from the reference program's by a relative error of at most 0.0085.
Values may be sent and summed in bfloat16 or wider, within the bound.
A program may use at most 128 MiB of HBM per device.

```python
import math
import jax
import jax.numpy as jnp
import numpy as np
from jax import lax

D = 4096
VOCAB = 32768
HEAD_NUMBER = 128
HEAD_DIM = 64
STATE = 128
GROUPS = 8
QBLK = 128
TOK_DEV = 256
TOKEN_POSITIONS = 2048
INNER = 8192


def draw_resid_out(key, part):
    values = jax.random.truncated_normal(jax.random.fold_in(key, 101), -4.0, 4.0, (TOKEN_POSITIONS, D), jnp.float32) * 0.25
    return values.astype(jnp.bfloat16)


def draw_head_weight(key, part):
    noise = jax.random.truncated_normal(jax.random.fold_in(key, 201), -4.0, 4.0, (D, VOCAB), jnp.float32)
    position = jnp.arange(VOCAB, dtype=jnp.float32) / VOCAB
    spread = jnp.exp(jax.random.uniform(jax.random.fold_in(key, 202), (VOCAB,), jnp.float32, 0.0, math.log(10.0)))
    column_scale = 0.25 * jnp.exp(math.log(3.0) * (position - 0.5)) * spread
    common = jax.random.truncated_normal(jax.random.fold_in(key, 203), -3.0, 3.0, (D, 1), jnp.float32)
    common_part = 2.0
    weights = (noise * column_scale[None, :] + common_part * common) / math.sqrt(D)
    return weights.astype(jnp.bfloat16)


def draw_log_decay(key, part):
    share = 0.5
    fast = jax.random.bernoulli(jax.random.fold_in(key, 301), share, (HEAD_NUMBER, 1))
    fast_rate = jnp.exp(jax.random.uniform(jax.random.fold_in(key, 302), (HEAD_NUMBER, 1), jnp.float32, math.log(0.02), math.log(0.035)))
    spike_probability = jnp.where(fast, fast_rate, 0.4 / TOKEN_POSITIONS)
    shard_count = TOKEN_POSITIONS // TOK_DEV
    block_factor = jnp.exp(jax.random.uniform(jax.random.fold_in(key, 303), (HEAD_NUMBER, shard_count, 1), jnp.float32, math.log(0.5), math.log(2.0)))
    rough = jnp.exp(jax.random.uniform(jax.random.fold_in(key, 304), (HEAD_NUMBER, shard_count, TOK_DEV), jnp.float32, math.log(0.5), math.log(2.0)))
    multiplier = (block_factor * rough).reshape(HEAD_NUMBER, TOKEN_POSITIONS)
    spike_positions = jax.random.randint(jax.random.fold_in(key, 305), (HEAD_NUMBER, 2), 0, TOKEN_POSITIONS)
    spike_length = jax.random.uniform(jax.random.fold_in(key, 306), (HEAD_NUMBER, 2), jnp.float32, math.log(0.5), math.log(0.8))
    spike_count = (jnp.arange(TOKEN_POSITIONS)[None, None, :] == spike_positions[:, :, None]).astype(jnp.float32)
    spike_events = jnp.sum(spike_count * spike_length[:, :, None], axis=1)
    return -(spike_probability * multiplier) + spike_events


def plant(entries, own_key, smallest, largest):
    place = [jax.random.randint(jax.random.fold_in(own_key, axis), (), 0, length) for axis, length in enumerate(entries.shape)]
    widest = entries.shape.index(max(entries.shape))
    next_to = place[:widest] + [(place[widest] + 1) % entries.shape[widest]] + place[widest + 1:]
    return entries.at[tuple(place)].set(smallest).at[tuple(next_to)].set(largest)


def block_levels(stream_key, dims, shards, smallest, high):
    gain = 1.0
    for axis_at, parts in shards:
        steps = jax.random.uniform(jax.random.fold_in(jax.random.fold_in(stream_key, 6), axis_at), (parts,), jnp.float32, smallest / len(shards), high / len(shards))
        gain = gain * jnp.repeat(jnp.exp(steps), dims[axis_at] // parts).reshape((-1,) + (1,) * (len(dims) - 1 - axis_at))
    return gain


def cumulative_ranks(number_of, lean):
    portions = [(1 << 20) // math.isqrt(rank ** lean) + 1 for rank in range(1, number_of + 1)]
    scale = 1 + sum(portions) // (1 << 30)
    return np.cumsum(np.array([max(1, weight // scale) for weight in portions]))


def skewed_ids(own_key, shape, number_of, slope):
    listing = cumulative_ranks(number_of, slope)
    lot = jax.random.randint(jax.random.fold_in(own_key, 1), shape, 0, int(listing[number_of - 1]))
    rank = jnp.searchsorted(jnp.asarray(listing, jnp.int32), lot, side="right")
    return jax.random.permutation(jax.random.fold_in(own_key, 2), number_of)[rank].astype(jnp.int32)


def normal_values(rng, dims, scale, limit, shards=(), kind=jnp.bfloat16):
    gain = block_levels(rng, dims, shards, -0.22, 0.18) if shards else 1.0
    array = jax.random.normal(rng, dims, jnp.float32) * scale * gain
    return jnp.minimum(jnp.maximum(array, -limit), limit).astype(kind)


def setup_inputs(seed: int = 0) -> dict:
    seeds = jax.random.split(jax.random.key(seed), 14)
    resid_out = draw_resid_out(jax.random.fold_in(seeds[13], 71), 0)
    final_gain = jnp.clip(1.0 + 0.1 * jax.random.normal(seeds[1], (D,), jnp.float32), 0.5, 1.5)
    head_weight = draw_head_weight(jax.random.fold_in(seeds[13], 71), 0)
    targets = plant(skewed_ids(seeds[3], (TOKEN_POSITIONS,), VOCAB, 2), jax.random.fold_in(seeds[3], 3), 0, VOCAB - 1).astype(jnp.int32)
    out_weight = normal_values(seeds[4], (INNER, D), INNER ** -0.5, 0.0625, ((0, 32), (1, 8)))
    norm_gain = jnp.clip(1.0 + 0.1 * jax.random.normal(seeds[5], (INNER,), jnp.float32), 0.5, 1.5)
    xs = normal_values(seeds[6], (TOKEN_POSITIONS, INNER), 1.0, 6.0, ((0, 8), (1, 32)))
    gate_z = normal_values(seeds[7], (TOKEN_POSITIONS, INNER), 1.0, 6.0, ((0, 8), (1, 32)))
    b_proj = normal_values(seeds[8], (TOKEN_POSITIONS, GROUPS * STATE), 0.3, 1.796875, ((0, 8),))
    c_proj = normal_values(seeds[9], (TOKEN_POSITIONS, GROUPS * STATE), 0.3, 1.796875, ((0, 8),))
    step_dt = jnp.clip(jnp.exp(math.log(0.05) - 1.609438 * jax.random.uniform(seeds[10], (HEAD_NUMBER, TOKEN_POSITIONS), jnp.float32) ** block_levels(seeds[10], (HEAD_NUMBER, TOKEN_POSITIONS), ((0, 32), (1, 8)), -0.2, 0.2)), 0.01, 0.05)
    log_decay = draw_log_decay(jax.random.fold_in(seeds[13], 71), 0)
    skip_d = jnp.clip(0.5 + 1.0 * jax.random.uniform(seeds[12], (HEAD_NUMBER,), jnp.float32) ** block_levels(seeds[12], (HEAD_NUMBER,), ((0, 32),), -0.2, 0.2), 0.5, 1.5)
    return {"resid_out": resid_out, "final_gain": final_gain, "head_weight": head_weight, "targets": targets, "out_weight": out_weight, "norm_gain": norm_gain, "xs": xs, "gate_z": gate_z, "b_proj": b_proj, "c_proj": c_proj, "step_dt": step_dt, "log_decay": log_decay, "skip_d": skip_d}


epsilon = 1e-05
precise = lax.Precision.HIGHEST

def block_update(carried, segment):
    x_block, step_block, decay_block, b_block, c_block = segment
    running = jnp.cumsum(decay_block, axis=1)
    length = decay_block.shape[1]
    causal = jnp.arange(length)[:, None] >= jnp.arange(length)[None, :]
    span_decay = jnp.exp(jnp.where(causal[None], running[:, :, None] - running[:, None, :], -jnp.inf))
    scores = jnp.einsum('thn,shn->hts', c_block, b_block, precision=precise) * span_decay * step_block[:, None, :]
    outputs = jnp.einsum('hts,shp->thp', scores, x_block, precision=precise)
    c_decayed = c_block * jnp.exp(running).T[:, :, None]
    outputs = outputs + jnp.einsum('thn,hnp->thp', c_decayed, carried, precision=precise)
    tail_weight = (jnp.exp(running[:, -1:] - running) * step_block).T
    update = jnp.einsum('shn,shp->hnp', b_block * tail_weight[:, :, None], x_block, precision=precise)
    new_carried = jnp.exp(running[:, -1])[:, None, None] * carried + update
    return (new_carried, outputs)

def run_ssd(x_heads, step_rows, decay_rows, b_heads, c_heads, start_state):
    positions, head_count, channels = x_heads.shape
    blocks = positions // QBLK

    def by_rows(values):
        return values.reshape(blocks, QBLK, head_count, values.shape[2])

    def by_heads(values):
        return values.reshape(head_count, blocks, QBLK).transpose(1, 0, 2)
    final_state, outputs = lax.scan(block_update, start_state, (by_rows(x_heads), by_heads(step_rows), by_heads(decay_rows), by_rows(b_heads), by_rows(c_heads)))
    return (outputs.reshape(positions, head_count, channels), final_state)

def select_heads(projection, selector):
    positions = projection.shape[0]
    return jnp.einsum('tgn,hg->thn', projection.reshape(positions, GROUPS, -1), selector, precision=precise)

def layer_core(x_float, step_rows, decay_rows, b_float, c_float, start_state, selector, skip_d):
    positions = x_float.shape[0]
    head_count = selector.shape[0]
    x_heads = x_float.reshape(positions, head_count, HEAD_DIM)
    outputs, final_state = run_ssd(x_heads, step_rows, decay_rows, select_heads(b_float, selector), select_heads(c_float, selector), start_state)
    outputs = outputs + skip_d[None, :, None] * x_heads
    return (outputs.reshape(positions, head_count * HEAD_DIM), final_state)

def reference(resid_out, final_gain, head_weight, targets, out_weight, norm_gain, xs, gate_z, b_proj, c_proj, step_dt, log_decay, skip_d):
    resid_float = resid_out.astype(jnp.float32)
    inv_rms = lax.rsqrt(lax.optimization_barrier(jnp.mean(resid_float * resid_float, axis=1, keepdims=True)) + epsilon)
    normed = (resid_float * inv_rms * final_gain[None, :]).astype(jnp.bfloat16)
    logits = jnp.dot(normed, head_weight, preferred_element_type=jnp.float32)
    row_max = lax.optimization_barrier(jnp.max(logits, axis=1))
    log_norm = row_max + jnp.log(lax.optimization_barrier(jnp.sum(jnp.exp(logits - row_max[:, None]), axis=1)))
    match = (targets[:, None] == jnp.arange(VOCAB, dtype=jnp.int32)[None, :]).astype(jnp.float32)
    grad_logits = (jnp.exp(logits - log_norm[:, None]) - match).astype(jnp.bfloat16)
    grad_head = jnp.dot(normed.T, grad_logits, preferred_element_type=jnp.float32).astype(jnp.bfloat16)
    stream_grad = lax.dot_general(grad_logits, head_weight, (((1,), (1,)), ((), ())), preferred_element_type=jnp.float32)
    scaled = stream_grad * final_gain[None, :]
    inner_dot = lax.optimization_barrier(jnp.sum(resid_float * scaled, axis=1))
    grad_resid = (inv_rms * scaled - resid_float * inv_rms * inv_rms * inv_rms * (inner_dot / D)[:, None]).astype(jnp.bfloat16)
    token_count = resid_out.shape[0]
    group_width = INNER // GROUPS
    selector = (jnp.arange(HEAD_NUMBER)[:, None] // (HEAD_NUMBER // GROUPS) == jnp.arange(GROUPS)[None, :]).astype(jnp.float32)
    start_state = jnp.zeros((HEAD_NUMBER, STATE, HEAD_DIM), jnp.float32)

    def core(x_in, step_in, decay_in, b_in, c_in):
        return layer_core(x_in, step_in, decay_in, b_in, c_in, start_state, selector, skip_d)[0]
    ssd_out, pullback = jax.vjp(core, xs.astype(jnp.float32), step_dt, log_decay, b_proj.astype(jnp.float32), c_proj.astype(jnp.float32))
    gate_float = gate_z.astype(jnp.float32)
    sigmoid = jax.nn.sigmoid(gate_float)
    gated = ssd_out * gate_float * sigmoid
    gated_heads = gated.reshape(token_count, HEAD_NUMBER, HEAD_DIM)
    group_sums = jnp.dot(lax.optimization_barrier(jnp.sum(gated_heads * gated_heads, axis=2)), selector, precision=precise)
    group_inv = lax.rsqrt(group_sums / group_width + epsilon)
    head_inv = jnp.dot(group_inv, selector.T, precision=precise)
    gain_heads = norm_gain.reshape(HEAD_NUMBER, HEAD_DIM)
    normed_inner = (gated_heads * head_inv[:, :, None] * gain_heads[None]).reshape(token_count, INNER).astype(jnp.bfloat16)
    grad_out_weight = jnp.dot(normed_inner.T, grad_resid, preferred_element_type=jnp.float32).astype(jnp.bfloat16)
    grad_normed = lax.dot_general(grad_resid, out_weight, (((1,), (1,)), ((), ())), preferred_element_type=jnp.float32)
    scaled_inner = grad_normed.reshape(token_count, HEAD_NUMBER, HEAD_DIM) * gain_heads[None]
    group_dot = jnp.dot(lax.optimization_barrier(jnp.sum(gated_heads * scaled_inner, axis=2)), selector, precision=precise)
    head_dot = jnp.dot(group_dot, selector.T, precision=precise)
    grad_gated = head_inv[:, :, None] * scaled_inner - gated_heads * (head_inv * head_inv * head_inv * head_dot / group_width)[:, :, None]
    grad_gated = grad_gated.reshape(token_count, INNER)
    grad_gate = (grad_gated * ssd_out * sigmoid * (1.0 + gate_float * (1.0 - sigmoid))).astype(jnp.bfloat16)
    grad_ssd = grad_gated * gate_float * sigmoid
    grad_x, grad_dt, grad_decay, grad_b, grad_c = pullback(grad_ssd)
    return (grad_head, grad_resid, grad_out_weight, grad_x.astype(jnp.bfloat16), grad_gate, grad_b.astype(jnp.bfloat16), grad_c.astype(jnp.bfloat16), grad_dt, grad_decay)
```

```python
import functools

import jax
import jax.numpy as jnp
from jax import lax
from jax.experimental import pallas as pl
from jax.experimental.pallas import tpu as pltpu
from jax.sharding import PartitionSpec as P

MESH = pl.DeviceIdType.MESH
F32 = jnp.float32
BF16 = jnp.bfloat16
D = 4096
INNER = 8192
GROUPS = 8
EPS = 1e-05
CTX = 8
VOC = 32
TOK = 256
HIGH = lax.Precision.HIGHEST
STATE_ROWS = 160
HALF = TOK // 2


def dot(a, b, ca=1, cb=0):
    return lax.dot_general(a, b, (((ca,), (cb,)), ((), ())), preferred_element_type=F32)


def dot_high(a, b, ca=1, cb=0):
    return lax.dot_general(
        a, b, (((ca,), (cb,)), ((), ())), precision=HIGH, preferred_element_type=F32
    )


def halves(a):
    high = a.astype(BF16)
    return high, (a - high.astype(F32)).astype(BF16)


def dot_left(a, b, ca=1, cb=0):
    high, low = halves(a)
    return dot(high, b, ca, cb) + dot(low, b, ca, cb)


def dot_right(a, b, ca=1, cb=0):
    high, low = halves(b)
    return dot(a, high, ca, cb) + dot(a, low, ca, cb)


def dot_both(a, b, ca=1, cb=0):
    ah, al = halves(a)
    bh, bl = halves(b)
    return dot(ah, bh, ca, cb) + (dot(al, bh, ca, cb) + dot(ah, bl, ca, cb))


def column(row):
    return jnp.broadcast_to(row, (128, row.shape[1])).T


def row_of(col):
    return col.T[0:1]


def wide(col, lanes):
    return jnp.concatenate([col] * (lanes // 128), axis=1)


def send(src, dst, ssem, rsem, device):
    copy = pltpu.make_async_remote_copy(
        src_ref=src, dst_ref=dst, send_sem=ssem, recv_sem=rsem, device_id=device, device_id_type=MESH
    )
    copy.start()


class Ctx:
    def __init__(self, buf, ssem, rsem, c):
        y, k = c // 2, c % 2
        self.buf, self.s, self.r, self.c = buf, ssem, rsem, c
        at = lambda dy, kk: ((y + dy) % 4) * 2 + kk
        self.own, self.yp, self.ym, self.y2 = c, at(1, k), at(3, k), at(2, k)
        self.sib, self.syp, self.sym, self.sy2 = at(0, 1 - k), at(1, 1 - k), at(3, 1 - k), at(2, 1 - k)
        rows = buf.shape[1]
        self.top, self.bottom = pl.ds(0, rows // 2), pl.ds(rows // 2, rows // 2)

    def ref(self, block, part=None):
        return self.buf.at[block] if part is None else self.buf.at[block, part]

    def go(self, slot, block, to, part=None):
        ref = self.ref(block, part)
        send(ref, ref, self.s.at[slot], self.r.at[slot], {"ctx": to})

    def got(self, slot, block, part=None):
        ref = self.ref(block, part)
        pltpu.make_async_remote_copy(
            src_ref=ref, dst_ref=ref, send_sem=self.s.at[slot], recv_sem=self.r.at[slot],
            device_id={"ctx": self.sib}, device_id_type=MESH,
        ).wait_recv()

    def sent(self, slot, block, part=None):
        ref = self.ref(block, part)
        pltpu.make_async_remote_copy(
            src_ref=ref, dst_ref=ref, send_sem=self.s.at[slot], recv_sem=self.r.at[slot],
            device_id={"ctx": self.sib}, device_id_type=MESH,
        ).wait_send()

    def start(self):
        self.go(0, self.own, self.yp)
        self.go(1, self.own, self.ym)
        self.go(2, self.own, self.sib)

    def middle(self):
        self.got(0, self.ym)
        self.go(5, self.ym, self.yp, self.top)
        self.go(3, self.ym, self.sib)
        self.got(1, self.yp)
        self.go(6, self.yp, self.ym, self.bottom)
        self.go(4, self.yp, self.sib)

    def end(self):
        self.got(5, self.y2, self.top)
        self.go(7, self.y2, self.sib, self.top)
        self.got(6, self.y2, self.bottom)
        self.go(8, self.y2, self.sib, self.bottom)

    def finish(self):
        self.got(2, self.sib)
        self.got(3, self.sym)
        self.got(4, self.syp)
        self.last()

    def last(self):
        self.got(7, self.sy2, self.top)
        self.got(8, self.sy2, self.bottom)

    def drain(self):
        self.sent(0, self.own)
        self.sent(1, self.own)
        self.sent(2, self.own)
        self.sent(3, self.ym)
        self.sent(4, self.yp)
        self.sent(5, self.ym, self.top)
        self.sent(6, self.yp, self.bottom)
        self.sent(7, self.y2, self.top)
        self.sent(8, self.y2, self.bottom)


ORDER = (0, 1, 7, 2, 6, 3, 5, 4)


class Voc:
    def __init__(self, buf, ssem, rsem, v):
        self.buf, self.s, self.r = buf, ssem, rsem
        self.x, self.z = v // 8, v % 8
        self.v = v
        self.xp, self.xm = (self.x + 1) % 4, (self.x + 3) % 4

    def wait(self, refs, sem_s, sem_r, receive):
        copy = pltpu.make_async_remote_copy(
            src_ref=refs, dst_ref=refs, send_sem=sem_s, recv_sem=sem_r,
            device_id={"vocab": self.xp * 8 + self.z}, device_id_type=MESH,
        )
        if receive:
            copy.wait_recv()
        else:
            copy.wait_send()

    def start(self):
        for d in ORDER[1:]:
            ref = self.buf.at[self.v]
            send(ref, ref, self.s.at[0], self.r.at[d], {"vocab": self.x * 8 + (self.z + d) % 8})

    def spread(self):
        for d in ORDER:
            ref = self.buf.at[self.x * 8 + (self.z + 8 - d) % 8]
            if d:
                self.wait(ref, self.s.at[0], self.r.at[d], True)
            send(ref, ref, self.s.at[1], self.r.at[8 + d], {"vocab": self.xp * 8 + self.z})
            send(ref, ref, self.s.at[2], self.r.at[16 + d], {"vocab": self.xm * 8 + self.z})

    def relay(self):
        for d in ORDER:
            zz = (self.z + 8 - d) % 8
            block = self.xm * 8 + zz
            self.wait(self.buf.at[block], self.s.at[1], self.r.at[8 + d], True)
            ref = self.buf.at[block, pl.ds(0, HALF)]
            send(ref, ref, self.s.at[3], self.r.at[24 + d], {"vocab": self.xp * 8 + self.z})
            block = self.xp * 8 + zz
            self.wait(self.buf.at[block], self.s.at[2], self.r.at[16 + d], True)
            ref = self.buf.at[block, pl.ds(HALF, HALF)]
            send(ref, ref, self.s.at[4], self.r.at[32 + d], {"vocab": self.xm * 8 + self.z})

    def finish(self):
        for d in ORDER:
            block = ((self.x + 2) % 4) * 8 + (self.z + 8 - d) % 8
            self.wait(self.buf.at[block, pl.ds(0, HALF)], self.s.at[3], self.r.at[24 + d], True)
            self.wait(self.buf.at[block, pl.ds(HALF, HALF)], self.s.at[4], self.r.at[32 + d], True)

    def drain(self):
        self.wait(self.buf.at[pl.ds(0, 7)], self.s.at[0], self.r.at[0], False)
        self.wait(self.buf.at[pl.ds(0, 8)], self.s.at[1], self.r.at[0], False)
        self.wait(self.buf.at[pl.ds(0, 8)], self.s.at[2], self.r.at[0], False)
        self.wait(self.buf.at[pl.ds(0, 4)], self.s.at[3], self.r.at[0], False)
        self.wait(self.buf.at[pl.ds(0, 4)], self.s.at[4], self.r.at[0], False)


class Many:
    def __init__(self, axis, me, peer, count, src, dst, ssem, rsem):
        self.axis, self.me, self.peer, self.count = axis, me, peer, count
        self.src, self.dst, self.ssem, self.rsem = src, dst, ssem, rsem

    def start(self, slot):
        @pl.loop(1, self.count)
        def _(d):
            to = self.peer(d)
            send(self.src(to), self.dst.at[slot], self.ssem, self.rsem, {self.axis: to})

    def whole(self):
        refs = self.dst.at[pl.ds(0, self.count - 1)]
        return pltpu.make_async_remote_copy(
            src_ref=refs, dst_ref=refs, send_sem=self.ssem, recv_sem=self.rsem,
            device_id={self.axis: self.peer(1)}, device_id_type=MESH,
        )

    def got(self):
        self.whole().wait_recv()

    def drain(self):
        self.whole().wait_send()


def kernel(*refs):
    (resid, gain, head_w, target, out_w, norm_gain, xs, gate, b_in, c_in, dt_in, decay_in, skip_in) = refs[:13]
    (gh_o, gr_o, gow_o, gx_o, gg_o, gb_o, gc_o, gdt_o, gld_o) = refs[13:22]
    (wbuf, owbuf, sbuf, nbuf, ntsend, ntbuf, logits, gall, pbuf, rel_a, rel_b, from_m, from_p, rz, gbuf,
     ubuf, vbuf, osend, obuf, es, acc, lse_b, inner_b, gsum_b, gdot_b, mean_s, mean_b, bcs, bcr, mcol, ycur, cbb, cb_ch0, gyb,
     lsem, ws, wr, ows, owr, gs, gr, us, ur, vs, vr, s1s, s1r, s2s, s2r, rs_s, rs_r, ms, mr) = refs[22:]
    c = lax.axis_index("ctx")
    v = lax.axis_index("vocab")
    x, z = v // 8, v % 8
    xp, xm, x2 = (x + 1) % 4, (x + 3) % 4, (x + 2) % 4

    barrier = pltpu.get_barrier_semaphore()

    @pl.loop(1, VOC)
    def _(d):
        pl.semaphore_signal(barrier, inc=1, device_id={"vocab": (v + d) % VOC}, device_id_type=MESH)

    @pl.loop(1, CTX)
    def _(d):
        pl.semaphore_signal(barrier, inc=1, device_id={"ctx": (c + d) % CTX}, device_id_type=MESH)

    local = [
        pltpu.make_async_copy(resid, sbuf.at[v], lsem.at[0]),
        pltpu.make_async_copy(head_w, wbuf.at[c], lsem.at[1]),
        pltpu.make_async_copy(out_w, owbuf.at[c], lsem.at[2]),
    ]
    for copy in local:
        copy.start()
    for copy in local:
        copy.wait()
    pl.semaphore_wait(barrier, VOC + CTX - 2)

    weights = Ctx(wbuf, ws, wr, c)
    outs_w = Ctx(owbuf, ows, owr, c)
    grads = Ctx(gall, gs, gr, c)
    states = Ctx(ubuf, us, ur, c)
    adjoints = Ctx(vbuf, vs, vr, c)
    stream = Voc(sbuf, s1s, s1r, v)
    back = Voc(gbuf, s2s, s2r, v)
    over_v = lambda d: (v + d) % VOC
    over_c = lambda d: (c + d) % CTX
    quarter = (v // 4) * 4
    over_g = lambda d: quarter + (v % 4 + d) % 4
    lse_x = Many("vocab", v, over_v, VOC, lambda to: lse_b.at[v], lse_b, ms.at[0], mr.at[0])
    inner_x = Many("vocab", v, over_v, VOC, lambda to: inner_b.at[v], inner_b, ms.at[1], mr.at[1])
    gsum_x = Many("vocab", v, over_g, 4, lambda to: gsum_b.at[v % 4], gsum_b, ms.at[2], mr.at[2])
    gdot_x = Many("vocab", v, over_g, 4, lambda to: gdot_b.at[v % 4], gdot_b, ms.at[3], mr.at[3])
    norm_x = Many("ctx", c, over_c, CTX, lambda to: ntsend.at[to], ntbuf, ms.at[4], mr.at[4])
    out_x = Many("ctx", c, over_c, CTX, lambda to: osend.at[to], obuf, ms.at[5], mr.at[5])
    bc_x = Many("vocab", v, over_v, VOC, lambda to: bcs.at[to], bcr, ms.at[6], mr.at[6])
    mean_x = Many("vocab", v, over_v, VOC, lambda to: mean_s.at[to], mean_b, ms.at[7], mr.at[7])

    stream.start()
    weights.start()
    stream.spread()

    group = v // 4
    lanes = pl.ds(pl.multiple_of(group * 128, 128), 128)
    b = b_in[:, lanes]
    cc = c_in[:, lanes]
    xb = xs[...]
    xf = xb.astype(F32)
    row_i = lax.broadcasted_iota(jnp.int32, (TOK, TOK), 0)
    col_i = lax.broadcasted_iota(jnp.int32, (TOK, TOK), 1)
    upper = (row_i <= col_i).astype(F32)
    head_of = lax.broadcasted_iota(jnp.int32, (8, TOK), 1) // 64
    sel = (head_of == lax.broadcasted_iota(jnp.int32, (8, TOK), 0)).astype(F32)
    dt = dt_in[...]
    a = dot_high(decay_in[...], upper)
    last = a[:, TOK - 1 :]
    tail = jnp.exp(last - a) * dt
    a_cols = jnp.concatenate([a] * 16, axis=0).T
    cbb[...] = dot(cc, b, 1, 1)
    low = lax.broadcasted_iota(jnp.int32, (TOK, 128), 1) < 64
    for pair in range(2):
        outs = []
        for h in (2 * pair, 2 * pair + 1):
            gap = a_cols[:, h : h + 1] - a[h : h + 1]
            e = jnp.exp(jnp.where(row_i >= col_i, gap, -1e30)) * dt[h : h + 1]
            es[h] = e
            outs.append(dot_left(cbb[...] * e, xb[:, pair * 128 : pair * 128 + 128]))
        ycur[:, pair * 128 : pair * 128 + 128] = jnp.where(low, outs[0], outs[1])
    tail_full = dot_high(tail, sel, 0, 0)
    grow_full = dot_high(jnp.exp(a), sel, 0, 0)
    ubuf[c, 0:128] = dot_right(b, tail_full * xf, 0, 0)
    whole = dot_high(jnp.broadcast_to(jnp.exp(last), (8, 128)), sel, 0, 0)
    ubuf[c, 128:STATE_ROWS] = whole[0 : STATE_ROWS - 128]

    stream.relay()
    weights.middle()
    stream.finish()

    def square(i, total):
        block = sbuf[i].astype(F32)
        return total + block * block

    total = lax.fori_loop(0, VOC, square, jnp.zeros((TOK, 128), F32))
    inv = lax.rsqrt(jnp.sum(total, axis=1, keepdims=True) * (1.0 / D) + EPS)
    inv = jnp.broadcast_to(inv, (TOK, 128))

    @pl.loop(0, CTX)
    def _(i):
        parts = []
        for j in range(4):
            parts.append((sbuf[4 * i + j].astype(F32) * inv * gain[4 * i + j]).astype(BF16))
        block = jnp.concatenate(parts, axis=1)
        nbuf[i] = block
        ntsend[i] = block.T

    ntbuf[c] = ntsend[c]

    def logit(i, first=False):
        part = dot(nbuf[i], wbuf[i])
        if first:
            logits[...] = part
        else:
            logits[...] += part

    logit(weights.own, True)
    weights.got(2, weights.sib)
    logit(weights.sib)
    logit(weights.ym)
    logit(weights.yp)
    weights.end()
    logit(weights.y2)
    weights.got(3, weights.sym)
    logit(weights.sym)
    weights.got(4, weights.syp)
    logit(weights.syp)
    weights.last()
    logit(weights.sy2)

    states.start()
    outs_w.start()
    norm_x.start(c)

    @pl.loop(0, 4)
    def _(i):
        rows = pl.ds(pl.multiple_of(i * 64, 64), 64)
        part = logits[rows, :]
        most = jnp.max(part, axis=1, keepdims=True)
        value = most + jnp.log(jnp.sum(jnp.exp(part - most), axis=1, keepdims=True))
        mcol[rows, :] = jnp.broadcast_to(value, (64, 128))

    lse_b[v] = row_of(mcol[...])
    lse_x.start(v)
    target_col = column(target[...])
    states.middle()
    lse_x.got()
    every = lse_b[...]
    most = jnp.max(every, axis=0)
    log_norm = most + jnp.log(jnp.sum(jnp.exp(every - most[None]), axis=0))
    mcol[...] = column(log_norm)
    cb_ch0[:, 0:128] = target_col

    base = (v * 1024).astype(F32)
    ids = lax.broadcasted_iota(jnp.int32, (64, 1024), 1).astype(F32) + base

    @pl.loop(0, 4)
    def _(i):
        rows = pl.ds(pl.multiple_of(i * 64, 64), 64)
        part = logits[rows, :]
        hit = jnp.where(wide(cb_ch0[rows, 0:128], 1024) == ids, 1.0, 0.0)
        g = (jnp.exp(part - wide(mcol[rows, :], 1024)) - hit).astype(BF16)
        gall[c, rows, :] = g
        value = jnp.sum(g.astype(F32) * part, axis=1, keepdims=True)
        mcol[rows, :] = jnp.broadcast_to(value, (64, 128))
        value = jnp.sum(g.astype(F32), axis=1, keepdims=True)
        cb_ch0[rows, 128:256] = jnp.broadcast_to(value, (64, 128))

    inner_b[v, 0:1] = row_of(mcol[...])
    inner_b[v, 1:2] = row_of(cb_ch0[:, 128:256])
    inner_x.start(v)

    weigh = jnp.concatenate([gall[c], jnp.full((16, 1024), 2.0**-10, BF16)], axis=0)
    sums_g = cb_ch0[:, 128:256]

    def partial(i):
        part = dot(weigh, wbuf[i], 1, 1)
        for j in range(4):
            mean = part[TOK : TOK + 1, j * 128 : j * 128 + 128]
            mean_s[4 * i + j] = mean
            pbuf[4 * i + j] = (part[0:TOK, j * 128 : j * 128 + 128] - sums_g * mean).astype(BF16)

    rs = lambda i: (rs_s.at[i], rs_r.at[i])
    to_p, to_m = {"vocab": xp * 8 + z}, {"vocab": xm * 8 + z}

    def rs_wait(ref, i, receive=True):
        copy = pltpu.make_async_remote_copy(
            src_ref=ref, dst_ref=ref, send_sem=rs_s.at[i], recv_sem=rs_r.at[i], device_id=to_p, device_id_type=MESH
        )
        if receive:
            copy.wait_recv()
        else:
            copy.wait_send()

    top, bottom = pl.ds(0, HALF), pl.ds(HALF, HALF)
    far, near = 1 - z // 4, z // 4
    for n, h in enumerate((far, near)):
        partial(2 * x2 + h)
        four = pl.ds(4 * (2 * x2 + h), 4)
        send(pbuf.at[four, top], rel_a.at[n], *rs(n), to_p)
        send(pbuf.at[four, bottom], rel_b.at[n], *rs(2 + n), to_m)
    grads.start()
    for n, h in enumerate((far, near)):
        partial(2 * xp + h)
        partial(2 * xm + h)
    for n, h in enumerate((far, near)):
        partial(2 * x + h)
    mean_b[v] = mean_s[v]
    mean_x.start(v)
    states.end()
    outs_w.middle()
    for n, h in enumerate((far, near)):
        rs_wait(rel_a.at[n], n)
        for j in range(4):
            i = 4 * (2 * xp + h) + j
            pbuf[i, 0:HALF] = (pbuf[i, 0:HALF].astype(F32) + rel_a[n, j].astype(F32)).astype(BF16)
        send(pbuf.at[pl.ds(4 * (2 * xp + h), 4)], from_m.at[n], *rs(4 + n), to_p)
        rs_wait(rel_b.at[n], 2 + n)
        for j in range(4):
            i = 4 * (2 * xm + h) + j
            pbuf[i, HALF:TOK] = (pbuf[i, HALF:TOK].astype(F32) + rel_b[n, j].astype(F32)).astype(BF16)
        send(pbuf.at[pl.ds(4 * (2 * xm + h), 4)], from_p.at[n], *rs(6 + n), to_m)

    states.finish()

    def enter(j, h0):
        new = ubuf[j, 128:129] * h0 + ubuf[j, 0:128]
        return jnp.where(j < c, new, h0)

    h0 = lax.fori_loop(0, CTX - 1, enter, jnp.zeros((128, TOK), F32))
    vbuf[c, 0:128] = h0
    ch0 = dot_right(cc, h0) * grow_full
    cb_ch0[...] = ch0
    y = ycur[...] + ch0 + skip_in[...] * xf
    ycur[...] = y
    zf = gate[...].astype(F32)
    sig = 1.0 / (1.0 + jnp.exp(-zf))
    gated = y * zf * sig
    squares = dot_high(jnp.ones((8, TOK), F32), gated * gated, 1, 1)
    gsum_b[v % 4] = squares[0:1]
    gsum_x.start(v % 4)

    for n, h in enumerate((far, near)):
        rs_wait(from_m.at[n], 4 + n)
        rs_wait(from_p.at[n], 6 + n)
        for j in range(4):
            i = 4 * (2 * x + h) + j
            total = pbuf[i].astype(F32) + from_m[n, j].astype(F32) + from_p[n, j].astype(F32)
            pbuf[i] = total.astype(BF16)
        if n == 0:
            for j in range(4):
                zz = 4 * h + j
                send(pbuf.at[x * 8 + zz], rz.at[z], rs_s.at[8], rs_r.at[8], {"vocab": x * 8 + zz})
        else:
            for d in range(1, 4):
                zz = 4 * h + (z % 4 + d) % 4
                send(pbuf.at[x * 8 + zz], rz.at[z], rs_s.at[8], rs_r.at[8], {"vocab": x * 8 + zz})
    rz[z] = pbuf[v]
    grads.middle()
    outs_w.end()
    inner_x.got()
    inner = column(jnp.sum(inner_b[...], axis=0)[0:1])
    mean_x.got()
    extra = dot_high(inner_b[:, 1, :], mean_b[:, 0, :], 0, 0)
    resid_f = sbuf[v].astype(F32)
    less = resid_f * (inv * inv * inner * (1.0 / D))
    gsum_x.got()
    sums = jnp.sum(gsum_b[...], axis=0)
    ginv = column(lax.rsqrt(sums * (1.0 / (INNER // GROUPS)) + EPS))
    ginv = wide(ginv, TOK)
    ng = norm_gain[...]
    normed_t = (gated * ginv * ng).astype(BF16).T

    rs_wait(rz.at[pl.ds(0, 7)], 8)
    total = extra
    for j in range(8):
        total = total + rz[j].astype(F32)
    mine = (inv * (total * gain[v]) - less).astype(BF16)
    gr_o[...] = mine
    gbuf[v] = mine
    back.start()
    back.spread()

    grads.end()
    outs_w.finish()
    grads.finish()
    norm_x.got()
    acc[...] = jnp.zeros_like(acc)

    @pl.loop(0, 4)
    def _(i):
        acc[...] += dot(ntbuf[i], gall[i])

    back.relay()

    @pl.loop(4, CTX)
    def _(i):
        acc[...] += dot(ntbuf[i], gall[i])

    gh_o[...] = acc[...].astype(BF16)
    back.finish()

    def project(i, total):
        lhs = jnp.concatenate([gbuf[4 * i + j] for j in range(4)], axis=1)
        osend[i] = dot(normed_t, lhs).astype(BF16)
        return total + dot(lhs, owbuf[i], 1, 1)

    grad_normed = lax.fori_loop(0, CTX, project, jnp.zeros((TOK, TOK), F32))
    scaled = grad_normed * ng
    dots = dot_high(jnp.ones((8, TOK), F32), gated * scaled, 1, 1)
    gdot_b[v % 4] = dots[0:1]
    gdot_x.start(v % 4)
    out_x.start(c)
    obuf[c] = osend[c]
    gdot_x.got()
    gdot = wide(column(jnp.sum(gdot_b[...], axis=0)), TOK)
    grad_gated = ginv * scaled - gated * (ginv * ginv * ginv * gdot * (1.0 / (INNER // GROUPS)))
    gg_o[...] = (grad_gated * y * sig * (1.0 + zf * (1.0 - sig))).astype(BF16)
    gy = grad_gated * zf * sig
    gyb[...] = gy
    gye = gy * grow_full
    h0 = vbuf[c, 0:128]
    dc = dot_both(gye, h0, 1, 1)
    vbuf[c, 0:128] = dot_right(cc, gye, 0, 0)
    vbuf[c, 128:STATE_ROWS] = jnp.zeros((STATE_ROWS - 128, TOK), F32)
    adjoints.start()

    ones8 = jnp.ones((8, TOK), F32)
    dcb = jnp.zeros((TOK, TOK), F32)
    rows_m, cols_m = [], []
    for h in range(4):
        if h == 2:
            adjoints.middle()
        pair = h // 2
        gyp = gyb[:, pair * 128 : pair * 128 + 128]
        gym = jnp.where(low if h % 2 == 0 else jnp.logical_not(low), gyp, 0.0)
        e = es[h]
        s = cbb[...] * e
        ds = dot_left(gym, xb[:, pair * 128 : pair * 128 + 128], 1, 1)
        dcb = dcb + ds * e
        m = ds * s
        rows_m.append(dot_high(ones8, m, 1, 1)[0:1])
        cols_m.append(jnp.sum(m, axis=0, keepdims=True))
        part = dot_both(s, gym, 0, 0)
        if h % 2 == 0:
            held = part
        else:
            logits[:, pair * 128 : pair * 128 + 128] = held + part
    adjoints.end()
    zero4 = jnp.zeros((4, TOK), F32)
    rows_m = jnp.concatenate(rows_m + [zero4], axis=0)
    cols_m = jnp.concatenate(cols_m + [zero4], axis=0)
    dc = dc + dot_left(dcb, b)
    db = dot_left(dcb, cc, 0, 0)
    r_rows = dot_high(sel, gy * cb_ch0[...], 1, 1)
    adjoints.finish()

    def leave(j, h1):
        i = CTX - 1 - j
        new = ubuf[i, 128:129] * h1 + vbuf[i, 0:128]
        return jnp.where(i > c, new, h1)

    h1 = lax.fori_loop(0, CTX - 1, leave, jnp.zeros((128, TOK), F32))
    bdh = dot_right(b, h1) * tail_full
    gx_o[...] = (logits[:, 0:TOK] + skip_in[...] * gy + bdh).astype(BF16)
    db = db + dot_both(tail_full * xf, h1, 1, 1)
    bcs[:, 0] = db.reshape(VOC, 8, 128)
    bcs[:, 1] = dc.reshape(VOC, 8, 128)
    bcr[v] = bcs[v]
    bc_x.start(v)
    wq = dot_high(sel, bdh * xf, 1, 1)

    def again(j, h0):
        new = ubuf[j, 128:129] * h0 + ubuf[j, 0:128]
        return jnp.where(j < c, new, h0)

    h0 = lax.fori_loop(0, CTX - 1, again, jnp.zeros((128, TOK), F32))
    cross = jnp.sum(h0 * h1, axis=0, keepdims=True) * ubuf[c, 128:129]
    cross = dot_high(sel, jnp.broadcast_to(cross, (8, TOK)), 1, 1)[:, 0:1]
    gdt_o[...] = (cols_m + wq) / dt
    da = rows_m - cols_m + r_rows - wq
    at_end = cross + jnp.sum(wq, axis=1, keepdims=True)
    gld_o[...] = dot_high(da, (row_i >= col_i).astype(F32)) + at_end

    bc_x.got()
    for n, out in enumerate((gb_o, gc_o)):
        parts = []
        for g in range(GROUPS):
            parts.append((bcr[4 * g, n] + bcr[4 * g + 1, n]) + (bcr[4 * g + 2, n] + bcr[4 * g + 3, n]))
        out[...] = jnp.concatenate(parts, axis=1).astype(BF16)
    out_x.got()
    for j in range(4):
        cols = pl.ds(128 * j, 128)
        total = obuf[0, :, cols].astype(F32)
        for i in range(1, CTX):
            total = total + obuf[i, :, cols].astype(F32)
        gow_o[:, cols] = total.astype(BF16)

    for gather in (weights, outs_w, grads, states, adjoints):
        gather.drain()
    stream.drain()
    back.drain()
    for many in (lse_x, inner_x, gsum_x, gdot_x, norm_x, out_x, bc_x, mean_x):
        many.drain()
    for n in range(2):
        rs_wait(rel_a.at[n], n, False)
        rs_wait(rel_b.at[n], 2 + n, False)
        rs_wait(from_m.at[n], 4 + n, False)
        rs_wait(from_p.at[n], 6 + n, False)
    rs_wait(rz.at[pl.ds(0, 7)], 8, False)


def shards(resid, gain, head_w, targets, out_w, norm_gain, xs, gate, b, c, dt, decay, skip):
    heads = skip.shape[0]
    pad = lambda rows, fill: jnp.pad(rows, ((0, 8 - heads), (0, 0)), constant_values=fill)
    args = (
        resid,
        gain.reshape(VOC, 1, 128),
        head_w,
        targets.astype(F32).reshape(1, TOK),
        out_w,
        norm_gain.reshape(1, TOK),
        xs,
        gate,
        b,
        c,
        pad(dt, 1.0),
        pad(decay, 0.0),
        jnp.repeat(skip, TOK // heads).reshape(1, TOK),
    )
    vm = pl.BlockSpec(memory_space=pltpu.VMEM)
    hbm = pl.BlockSpec(memory_space=pl.ANY)
    shape = jax.ShapeDtypeStruct
    dma = pltpu.SemaphoreType.DMA
    scratch = [
        pltpu.VMEM((CTX, 512, 1024), BF16),
        pltpu.VMEM((CTX, TOK, 512), BF16),
        pltpu.VMEM((VOC, TOK, 128), BF16),
        pltpu.VMEM((CTX, TOK, 512), BF16),
        pltpu.VMEM((CTX, 512, TOK), BF16),
        pltpu.VMEM((CTX, 512, TOK), BF16),
        pltpu.VMEM((TOK, 1024), F32),
        pltpu.VMEM((CTX, TOK, 1024), BF16),
        pltpu.VMEM((VOC, TOK, 128), BF16),
        pltpu.VMEM((2, 4, HALF, 128), BF16),
        pltpu.VMEM((2, 4, HALF, 128), BF16),
        pltpu.VMEM((2, 4, TOK, 128), BF16),
        pltpu.VMEM((2, 4, TOK, 128), BF16),
        pltpu.VMEM((8, TOK, 128), BF16),
        pltpu.VMEM((VOC, TOK, 128), BF16),
        pltpu.VMEM((CTX, STATE_ROWS, TOK), F32),
        pltpu.VMEM((CTX, STATE_ROWS, TOK), F32),
        pltpu.VMEM((CTX, TOK, 512), BF16),
        pltpu.VMEM((CTX, TOK, 512), BF16),
        pltpu.VMEM((4, TOK, TOK), F32),
        pltpu.VMEM((512, 1024), F32),
        pltpu.VMEM((VOC, 1, TOK), F32),
        pltpu.VMEM((VOC, 2, TOK), F32),
        pltpu.VMEM((4, 1, TOK), F32),
        pltpu.VMEM((4, 1, TOK), F32),
        pltpu.VMEM((VOC, 1, 128), F32),
        pltpu.VMEM((VOC, 1, 128), F32),
        pltpu.VMEM((VOC, 2, 8, 128), F32),
        pltpu.VMEM((VOC, 2, 8, 128), F32),
        pltpu.VMEM((TOK, 128), F32),
        pltpu.VMEM((TOK, TOK), F32),
        pltpu.VMEM((TOK, TOK), F32),
        pltpu.VMEM((TOK, TOK), F32),
        pltpu.VMEM((TOK, TOK), F32),
        dma((3,)),
        dma((9,)), dma((9,)), dma((9,)), dma((9,)), dma((9,)), dma((9,)), dma((9,)), dma((9,)), dma((9,)), dma((9,)),
        dma((5,)), dma((40,)), dma((5,)), dma((40,)),
        dma((9,)), dma((9,)),
        dma((8,)), dma((8,)),
    ]
    outs = pl.pallas_call(
        kernel,
        out_shape=(
            shape((512, 1024), BF16),
            shape((TOK, 128), BF16),
            shape((TOK, 512), BF16),
            shape((TOK, TOK), BF16),
            shape((TOK, TOK), BF16),
            shape((8, 1024), BF16),
            shape((8, 1024), BF16),
            shape((8, TOK), F32),
            shape((8, TOK), F32),
        ),
        in_specs=[hbm, vm, hbm, vm, hbm] + [vm] * 8,
        out_specs=(vm,) * 9,
        scratch_shapes=scratch,
        compiler_params=pltpu.CompilerParams(
            collective_id=0, has_side_effects=True, vmem_limit_bytes=67043328
        ),
        name="step",
    )(*args)
    return outs[:7] + (outs[7][:heads], outs[8][:heads])


def solution(mesh):
    return jax.shard_map(
        shards,
        mesh=mesh,
        in_specs=(
            P("ctx", "vocab"),
            P(),
            P("ctx", "vocab"),
            P("ctx"),
            P("vocab", "ctx"),
            P("vocab"),
            P("ctx", "vocab"),
            P("ctx", "vocab"),
            P("ctx", None),
            P("ctx", None),
            P("vocab", "ctx"),
            P("vocab", "ctx"),
            P("vocab"),
        ),
        out_specs=(
            P("ctx", "vocab"),
            P("ctx", "vocab"),
            P("vocab", "ctx"),
            P("ctx", "vocab"),
            P("ctx", "vocab"),
            P(("ctx", "vocab"), None),
            P(("ctx", "vocab"), None),
            P("vocab", "ctx"),
            P("vocab", "ctx"),
        ),
        check_vma=False,
    )
```

```python
import functools

import jax
import jax.numpy as jnp
from jax import lax
from jax.experimental import pallas as pl
from jax.experimental.pallas import tpu as pltpu
from jax.sharding import PartitionSpec as P

MESH = pl.DeviceIdType.MESH
F32 = jnp.float32
BF16 = jnp.bfloat16
D = 4096
INNER = 8192
GROUPS = 8
EPS = 1e-05
CTX = 8
VOC = 32
TOK = 256
HIGH = lax.Precision.HIGHEST
STATE_ROWS = 160
HALF = TOK // 2


def dot(a, b, ca=1, cb=0):
    return lax.dot_general(a, b, (((ca,), (cb,)), ((), ())), preferred_element_type=F32)


def dot_high(a, b, ca=1, cb=0):
    return lax.dot_general(
        a, b, (((ca,), (cb,)), ((), ())), precision=HIGH, preferred_element_type=F32
    )


def halves(a):
    high = a.astype(BF16)
    return high, (a - high.astype(F32)).astype(BF16)


def dot_left(a, b, ca=1, cb=0):
    high, low = halves(a)
    return dot(high, b, ca, cb) + dot(low, b, ca, cb)


def dot_right(a, b, ca=1, cb=0):
    high, low = halves(b)
    return dot(a, high, ca, cb) + dot(a, low, ca, cb)


def dot_both(a, b, ca=1, cb=0):
    ah, al = halves(a)
    bh, bl = halves(b)
    return dot(ah, bh, ca, cb) + (dot(al, bh, ca, cb) + dot(ah, bl, ca, cb))


def column(row):
    return jnp.broadcast_to(row, (128, row.shape[1])).T


def row_of(col):
    return col.T[0:1]


def wide(col, lanes):
    return jnp.concatenate([col] * (lanes // 128), axis=1)


def send(src, dst, ssem, rsem, device):
    copy = pltpu.make_async_remote_copy(
        src_ref=src, dst_ref=dst, send_sem=ssem, recv_sem=rsem, device_id=device, device_id_type=MESH
    )
    copy.start()


class Ctx:
    def __init__(self, buf, ssem, rsem, c):
        y, k = c // 2, c % 2
        self.buf, self.s, self.r, self.c = buf, ssem, rsem, c
        at = lambda dy, kk: ((y + dy) % 4) * 2 + kk
        self.own, self.yp, self.ym, self.y2 = c, at(1, k), at(3, k), at(2, k)
        self.sib, self.syp, self.sym, self.sy2 = at(0, 1 - k), at(1, 1 - k), at(3, 1 - k), at(2, 1 - k)
        rows = buf.shape[1]
        self.top, self.bottom = pl.ds(0, rows // 2), pl.ds(rows // 2, rows // 2)

    def ref(self, block, part=None):
        return self.buf.at[block] if part is None else self.buf.at[block, part]

    def go(self, slot, block, to, part=None):
        ref = self.ref(block, part)
        send(ref, ref, self.s.at[slot], self.r.at[slot], {"ctx": to})

    def got(self, slot, block, part=None):
        ref = self.ref(block, part)
        pltpu.make_async_remote_copy(
            src_ref=ref, dst_ref=ref, send_sem=self.s.at[slot], recv_sem=self.r.at[slot],
            device_id={"ctx": self.sib}, device_id_type=MESH,
        ).wait_recv()

    def sent(self, slot, block, part=None):
        ref = self.ref(block, part)
        pltpu.make_async_remote_copy(
            src_ref=ref, dst_ref=ref, send_sem=self.s.at[slot], recv_sem=self.r.at[slot],
            device_id={"ctx": self.sib}, device_id_type=MESH,
        ).wait_send()

    def start(self):
        self.go(0, self.own, self.yp, self.top)
        self.go(1, self.own, self.ym, self.bottom)
        self.go(9, self.own, self.yp, self.bottom)
        self.go(10, self.own, self.ym, self.top)
        self.go(2, self.own, self.sib)

    def middle(self):
        self.got(0, self.ym, self.top)
        self.go(5, self.ym, self.yp, self.top)
        self.got(1, self.yp, self.bottom)
        self.go(6, self.yp, self.ym, self.bottom)
        self.got(9, self.ym, self.bottom)
        self.go(3, self.ym, self.sib)
        self.got(10, self.yp, self.top)
        self.go(4, self.yp, self.sib)

    def end(self):
        self.got(5, self.y2, self.top)
        self.go(7, self.y2, self.sib, self.top)
        self.got(6, self.y2, self.bottom)
        self.go(8, self.y2, self.sib, self.bottom)

    def finish(self):
        self.got(2, self.sib)
        self.got(3, self.sym)
        self.got(4, self.syp)
        self.last()

    def last(self):
        self.got(7, self.sy2, self.top)
        self.got(8, self.sy2, self.bottom)

    def drain(self):
        self.sent(0, self.own, self.top)
        self.sent(1, self.own, self.bottom)
        self.sent(9, self.own, self.bottom)
        self.sent(10, self.own, self.top)
        self.sent(2, self.own)
        self.sent(3, self.ym)
        self.sent(4, self.yp)
        self.sent(5, self.ym, self.top)
        self.sent(6, self.yp, self.bottom)
        self.sent(7, self.y2, self.top)
        self.sent(8, self.y2, self.bottom)


ORDER = (0, 1, 7, 2, 6, 3, 5, 4)
LAG = 3


class Voc:
    def __init__(self, buf, ssem, rsem, v):
        self.buf, self.s, self.r = buf, ssem, rsem
        self.x, self.z = v // 8, v % 8
        self.v = v
        self.xp, self.xm = (self.x + 1) % 4, (self.x + 3) % 4

    def wait(self, refs, sem_s, sem_r, receive):
        copy = pltpu.make_async_remote_copy(
            src_ref=refs, dst_ref=refs, send_sem=sem_s, recv_sem=sem_r,
            device_id={"vocab": self.xp * 8 + self.z}, device_id_type=MESH,
        )
        if receive:
            copy.wait_recv()
        else:
            copy.wait_send()

    def start(self):
        for d in ORDER[1:]:
            ref = self.buf.at[self.v]
            send(ref, ref, self.s.at[0], self.r.at[d], {"vocab": self.x * 8 + (self.z + d) % 8})

    def forward(self, d):
        ref = self.buf.at[self.x * 8 + (self.z + 8 - d) % 8]
        if d:
            self.wait(ref, self.s.at[0], self.r.at[d], True)
        send(ref, ref, self.s.at[1], self.r.at[8 + d], {"vocab": self.xp * 8 + self.z})
        send(ref, ref, self.s.at[2], self.r.at[16 + d], {"vocab": self.xm * 8 + self.z})

    def pass_on(self, d):
        zz = (self.z + 8 - d) % 8
        block = self.xm * 8 + zz
        self.wait(self.buf.at[block], self.s.at[1], self.r.at[8 + d], True)
        ref = self.buf.at[block, pl.ds(0, HALF)]
        send(ref, ref, self.s.at[3], self.r.at[24 + d], {"vocab": self.xp * 8 + self.z})
        block = self.xp * 8 + zz
        self.wait(self.buf.at[block], self.s.at[2], self.r.at[16 + d], True)
        ref = self.buf.at[block, pl.ds(HALF, HALF)]
        send(ref, ref, self.s.at[4], self.r.at[32 + d], {"vocab": self.xm * 8 + self.z})

    def spread(self, first=0):
        for n in range(8):
            if n >= first:
                self.forward(ORDER[n])
            if n >= LAG:
                self.pass_on(ORDER[n - LAG])

    def relay(self):
        for n in range(8 - LAG, 8):
            self.pass_on(ORDER[n])

    def finish(self):
        for d in ORDER:
            block = ((self.x + 2) % 4) * 8 + (self.z + 8 - d) % 8
            self.wait(self.buf.at[block, pl.ds(0, HALF)], self.s.at[3], self.r.at[24 + d], True)
            self.wait(self.buf.at[block, pl.ds(HALF, HALF)], self.s.at[4], self.r.at[32 + d], True)

    def drain(self):
        self.wait(self.buf.at[pl.ds(0, 7)], self.s.at[0], self.r.at[0], False)
        self.wait(self.buf.at[pl.ds(0, 8)], self.s.at[1], self.r.at[0], False)
        self.wait(self.buf.at[pl.ds(0, 8)], self.s.at[2], self.r.at[0], False)
        self.wait(self.buf.at[pl.ds(0, 4)], self.s.at[3], self.r.at[0], False)
        self.wait(self.buf.at[pl.ds(0, 4)], self.s.at[4], self.r.at[0], False)


class Many:
    def __init__(self, axis, me, peer, count, src, dst, ssem, rsem):
        self.axis, self.me, self.peer, self.count = axis, me, peer, count
        self.src, self.dst, self.ssem, self.rsem = src, dst, ssem, rsem

    def start(self, slot):
        @pl.loop(1, self.count)
        def _(d):
            to = self.peer(d)
            send(self.src(to), self.dst.at[slot], self.ssem, self.rsem, {self.axis: to})

    def whole(self):
        refs = self.dst.at[pl.ds(0, self.count - 1)]
        return pltpu.make_async_remote_copy(
            src_ref=refs, dst_ref=refs, send_sem=self.ssem, recv_sem=self.rsem,
            device_id={self.axis: self.peer(1)}, device_id_type=MESH,
        )

    def got(self):
        self.whole().wait_recv()

    def drain(self):
        self.whole().wait_send()


def kernel(*refs):
    (resid, gain, head_w, target, out_w, norm_gain, xs, gate, b_in, c_in, dt_in, decay_in, skip_in) = refs[:13]
    (gh_h, gr_h, gow_h, gx_h, gg_h, gb_o, gc_o, gdt_o, gld_o) = refs[13:22]
    (wbuf, owbuf, sbuf, nbuf, ntsend, ntbuf, logits, gall, pbuf, rel_a, rel_b, from_m, from_p, rz, gbuf,
     ubuf, vbuf, osend, obuf, es, acc, lse_b, inner_b, gsum_b, gdot_b, mean_s, mean_b, b_send, b_got, c_send, c_got, orel, xs_v, gate_v, b_v, c_v, gh_o, gr_o, gow_o, gx_o, gg_o, mcol, ycur, cbb, cb_ch0, gyb,
     lsem, ws, wr, ows, owr, gs, gr, us, ur, vs, vr, s1s, s1r, s2s, s2r, rs_s, rs_r, ms, mr, os_s, os_r) = refs[22:]
    c = lax.axis_index("ctx")
    v = lax.axis_index("vocab")
    x, z = v // 8, v % 8
    xp, xm, x2 = (x + 1) % 4, (x + 3) % 4, (x + 2) % 4

    lanes = pl.ds(pl.multiple_of((v // 4) * 128, 128), 128)
    barrier = pltpu.get_barrier_semaphore()

    @pl.loop(1, VOC)
    def _(d):
        pl.semaphore_signal(barrier, inc=1, device_id={"vocab": (v + d) % VOC}, device_id_type=MESH)

    @pl.loop(1, CTX)
    def _(d):
        pl.semaphore_signal(barrier, inc=1, device_id={"ctx": (c + d) % CTX}, device_id_type=MESH)

    local = [
        pltpu.make_async_copy(resid, sbuf.at[v], lsem.at[0]),
        pltpu.make_async_copy(head_w, wbuf.at[c], lsem.at[1]),
        pltpu.make_async_copy(out_w, owbuf.at[c], lsem.at[2]),
        pltpu.make_async_copy(xs, xs_v, lsem.at[3]),
        pltpu.make_async_copy(gate, gate_v, lsem.at[4]),
        pltpu.make_async_copy(b_in.at[:, lanes], b_v, lsem.at[5]),
        pltpu.make_async_copy(c_in.at[:, lanes], c_v, lsem.at[6]),
    ]
    for copy in local:
        copy.start()
    for copy in local[:2]:
        copy.wait()
    pl.semaphore_wait(barrier, VOC + CTX - 2)

    weights = Ctx(wbuf, ws, wr, c)
    outs_w = Ctx(owbuf, ows, owr, c)
    grads = Ctx(gall, gs, gr, c)
    states = Ctx(ubuf, us, ur, c)
    adjoints = Ctx(vbuf, vs, vr, c)
    stream = Voc(sbuf, s1s, s1r, v)
    back = Voc(gbuf, s2s, s2r, v)
    over_v = lambda d: (v + d) % VOC
    over_c = lambda d: (c + d) % CTX
    quarter = (v // 4) * 4
    over_g = lambda d: quarter + (v % 4 + d) % 4
    lse_x = Many("vocab", v, over_v, VOC, lambda to: lse_b.at[v], lse_b, ms.at[0], mr.at[0])
    inner_x = Many("vocab", v, over_v, VOC, lambda to: inner_b.at[v], inner_b, ms.at[1], mr.at[1])
    gsum_x = Many("vocab", v, over_g, 4, lambda to: gsum_b.at[v % 4], gsum_b, ms.at[2], mr.at[2])
    gdot_x = Many("vocab", v, over_g, 4, lambda to: gdot_b.at[v % 4], gdot_b, ms.at[3], mr.at[3])
    norm_x = Many("ctx", c, over_c, CTX, lambda to: ntsend.at[to], ntbuf, ms.at[4], mr.at[4])
    b_x = Many("vocab", v, over_v, VOC, lambda to: b_send.at[to], b_got, ms.at[6], mr.at[6])
    c_x = Many("vocab", v, over_v, VOC, lambda to: c_send.at[to], c_got, ms.at[5], mr.at[5])
    mean_x = Many("vocab", v, over_v, VOC, lambda to: mean_s.at[to], mean_b, ms.at[7], mr.at[7])

    puts = [
        pltpu.make_async_copy(src, dst, lsem.at[7 + n])
        for n, (src, dst) in enumerate(
            ((gh_o, gh_h), (gr_o, gr_h), (gow_o, gow_h), (gx_o, gx_h), (gg_o, gg_h))
        )
    ]
    stream.start()
    weights.start()
    stream.spread()

    for copy in local[2:]:
        copy.wait()
    b = b_v[...]
    cc = c_v[...]
    xb = xs_v[...]
    xf = xb.astype(F32)
    row_i = lax.broadcasted_iota(jnp.int32, (TOK, TOK), 0)
    col_i = lax.broadcasted_iota(jnp.int32, (TOK, TOK), 1)
    upper = (row_i <= col_i).astype(F32)
    head_of = lax.broadcasted_iota(jnp.int32, (8, TOK), 1) // 64
    sel = (head_of == lax.broadcasted_iota(jnp.int32, (8, TOK), 0)).astype(F32)
    dt = jnp.concatenate([dt_in[...], jnp.ones((4, TOK), F32)], axis=0)
    decay = jnp.concatenate([decay_in[...], jnp.zeros((4, TOK), F32)], axis=0)
    a = dot_high(decay, upper)
    last = a[:, TOK - 1 :]
    tail = jnp.exp(last - a) * dt
    a_cols = jnp.concatenate([a] * 16, axis=0).T
    cbb[...] = dot(cc, b, 1, 1)
    skip = jnp.zeros((1, TOK), F32)
    for h in range(4):
        skip = skip + sel[h : h + 1] * skip_in[h]
    low = lax.broadcasted_iota(jnp.int32, (TOK, 128), 1) < 64
    for pair in range(2):
        outs = []
        for h in (2 * pair, 2 * pair + 1):
            gap = a_cols[:, h : h + 1] - a[h : h + 1]
            e = jnp.exp(jnp.where(row_i >= col_i, gap, -1e30)) * dt[h : h + 1]
            es[h] = e
            outs.append(dot_left(cbb[...] * e, xb[:, pair * 128 : pair * 128 + 128]))
        ycur[:, pair * 128 : pair * 128 + 128] = jnp.where(low, outs[0], outs[1])
    tail_full = dot_high(tail, sel, 0, 0)
    grow_full = dot_high(jnp.exp(a), sel, 0, 0)
    ubuf[c, 0:128] = dot_right(b, tail_full * xf, 0, 0)
    whole = dot_high(jnp.broadcast_to(jnp.exp(last), (8, 128)), sel, 0, 0)
    ubuf[c, 128:STATE_ROWS] = whole[0 : STATE_ROWS - 128]

    stream.relay()
    weights.middle()
    stream.finish()

    def square(i, total):
        block = sbuf[i].astype(F32)
        return total + block * block

    total = lax.fori_loop(0, VOC, square, jnp.zeros((TOK, 128), F32))
    inv = lax.rsqrt(jnp.sum(total, axis=1, keepdims=True) * (1.0 / D) + EPS)
    inv = jnp.broadcast_to(inv, (TOK, 128))

    @pl.loop(0, CTX)
    def _(i):
        parts = []
        for j in range(4):
            parts.append((sbuf[4 * i + j].astype(F32) * inv * gain[4 * i + j]).astype(BF16))
        block = jnp.concatenate(parts, axis=1)
        nbuf[i] = block
        ntsend[i] = block.T

    ntbuf[c] = ntsend[c]

    def logit(i, first=False):
        part = dot(nbuf[i], wbuf[i])
        if first:
            logits[...] = part
        else:
            logits[...] += part

    logit(weights.own, True)
    weights.got(2, weights.sib)
    logit(weights.sib)
    logit(weights.ym)
    logit(weights.yp)
    weights.end()
    logit(weights.y2)
    weights.got(3, weights.sym)
    logit(weights.sym)
    weights.got(4, weights.syp)
    logit(weights.syp)
    weights.last()
    logit(weights.sy2)

    states.start()
    outs_w.start()

    @pl.loop(0, 4)
    def _(i):
        rows = pl.ds(pl.multiple_of(i * 64, 64), 64)
        part = logits[rows, :]
        most = jnp.max(part, axis=1, keepdims=True)
        value = most + jnp.log(jnp.sum(jnp.exp(part - most), axis=1, keepdims=True))
        mcol[rows, :] = jnp.broadcast_to(value, (64, 128))

    lse_b[v] = row_of(mcol[...])
    lse_x.start(v)
    target_col = column(target[...].astype(F32))
    lse_x.got()
    every = lse_b[...]
    most = jnp.max(every, axis=0)
    log_norm = most + jnp.log(jnp.sum(jnp.exp(every - most[None]), axis=0))
    mcol[...] = column(log_norm)
    cb_ch0[:, 0:128] = target_col

    base = (v * 1024).astype(F32)
    ids = lax.broadcasted_iota(jnp.int32, (64, 1024), 1).astype(F32) + base

    @pl.loop(0, 4)
    def _(i):
        rows = pl.ds(pl.multiple_of(i * 64, 64), 64)
        part = logits[rows, :]
        hit = jnp.where(wide(cb_ch0[rows, 0:128], 1024) == ids, 1.0, 0.0)
        g = (jnp.exp(part - wide(mcol[rows, :], 1024)) - hit).astype(BF16)
        gall[c, rows, :] = g
        value = jnp.sum(g.astype(F32) * part, axis=1, keepdims=True)
        mcol[rows, :] = jnp.broadcast_to(value, (64, 128))
        value = jnp.sum(g.astype(F32), axis=1, keepdims=True)
        cb_ch0[rows, 128:256] = jnp.broadcast_to(value, (64, 128))

    inner_b[v, 0:1] = row_of(mcol[...])
    inner_b[v, 1:2] = row_of(cb_ch0[:, 128:256])
    inner_x.start(v)

    top, bottom = pl.ds(0, HALF), pl.ds(HALF, HALF)

    weigh = jnp.concatenate([gall[c], jnp.full((16, 1024), 2.0**-10, BF16)], axis=0)
    sums_g = cb_ch0[:, 128:256]

    def partial(i):
        part = dot(weigh, wbuf[i], 1, 1)
        for j in range(4):
            mean = part[TOK : TOK + 1, j * 128 : j * 128 + 128]
            mean_s[4 * i + j] = mean
            pbuf[4 * i + j] = (part[0:TOK, j * 128 : j * 128 + 128] - sums_g * mean).astype(BF16)

    to_p, to_m = {"vocab": xp * 8 + z}, {"vocab": xm * 8 + z}

    def rs_send(kind, n, src, dst, to):
        send(src, dst, rs_s.at[kind], rs_r.at[8 * kind + n], to)

    def rs_wait(kind, n, ref, receive=True):
        copy = pltpu.make_async_remote_copy(
            src_ref=ref, dst_ref=ref, send_sem=rs_s.at[kind], recv_sem=rs_r.at[8 * kind + n],
            device_id=to_p, device_id_type=MESH,
        )
        if receive:
            copy.wait_recv()
        else:
            copy.wait_send()

    far, near = 1 - z // 4, z // 4
    serve = [4 * far + (z % 4 + 1 + j) % 4 for j in range(4)] + [4 * near + (z % 4 + 1 + j) % 4 for j in range(4)]
    for n in range(8):
        if n % 4 == 0:
            partial(2 * x2 + (far, near)[n // 4])
        rs_send(0, n, pbuf.at[x2 * 8 + serve[n], top], rel_a.at[n], to_p)
        rs_send(1, n, pbuf.at[x2 * 8 + serve[n], bottom], rel_b.at[n], to_m)
    grads.start()
    for h in (far, near):
        partial(2 * xp + h)
        partial(2 * xm + h)

    def relayed(n):
        rs_wait(0, n, rel_a.at[n])
        i = xp * 8 + serve[n]
        pbuf[i, 0:HALF] = (pbuf[i, 0:HALF].astype(F32) + rel_a[n].astype(F32)).astype(BF16)
        rs_send(2, n, pbuf.at[i], from_m.at[n], to_p)
        rs_wait(1, n, rel_b.at[n])
        i = xm * 8 + serve[n]
        pbuf[i, HALF:TOK] = (pbuf[i, HALF:TOK].astype(F32) + rel_b[n].astype(F32)).astype(BF16)
        rs_send(3, n, pbuf.at[i], from_p.at[n], to_m)

    for n in range(2):
        relayed(n)
    for h in (far, near):
        partial(2 * x + h)
    for n in range(2, 8):
        relayed(n)
    mean_b[v] = mean_s[v]
    mean_x.start(v)
    states.middle()
    outs_w.middle()
    norm_x.start(c)

    for n in range(8):
        rs_wait(2, n, from_m.at[n])
        rs_wait(3, n, from_p.at[n])
        i = x * 8 + serve[n]
        total = pbuf[i].astype(F32) + from_m[n].astype(F32) + from_p[n].astype(F32)
        pbuf[i] = total.astype(BF16)
        if n < 7:
            send(pbuf.at[i], rz.at[z], rs_s.at[4], rs_r.at[32], {"vocab": i})
    rz[z] = pbuf[v]
    states.end()
    outs_w.end()

    inner_x.got()
    inner = column(jnp.sum(inner_b[...], axis=0)[0:1])
    mean_x.got()
    extra = dot_high(inner_b[:, 1, :], mean_b[:, 0, :], 0, 0)
    resid_f = sbuf[v].astype(F32)
    less = resid_f * (inv * inv * inner * (1.0 / D))
    rs_wait(4, 0, rz.at[pl.ds(0, 7)])
    total = extra
    for j in range(8):
        total = total + rz[j].astype(F32)
    mine = (inv * (total * gain[v]) - less).astype(BF16)
    gr_o[...] = mine
    puts[1].start()
    gbuf[v] = mine
    back.start()
    back.forward(0)
    states.finish()

    def enter(j, h0):
        new = ubuf[j, 128:129] * h0 + ubuf[j, 0:128]
        return jnp.where(j < c, new, h0)

    h0 = lax.fori_loop(0, CTX - 1, enter, jnp.zeros((128, TOK), F32))
    vbuf[c, 0:128] = h0
    ch0 = dot_right(cc, h0) * grow_full
    cb_ch0[...] = ch0
    y = ycur[...] + ch0 + skip * xf
    ycur[...] = y
    zf = gate_v[...].astype(F32)
    sig = 1.0 / (1.0 + jnp.exp(-zf))
    gated = y * zf * sig
    squares = dot_high(jnp.ones((8, TOK), F32), gated * gated, 1, 1)
    gsum_b[v % 4] = squares[0:1]
    gsum_x.start(v % 4)

    back.spread(1)
    back.relay()
    gsum_x.got()
    sums = jnp.sum(gsum_b[...], axis=0)
    ginv = column(lax.rsqrt(sums * (1.0 / (INNER // GROUPS)) + EPS))
    ginv = wide(ginv, TOK)
    ng = norm_gain[...]
    normed_t = (gated * ginv * ng).astype(BF16).T
    outs_w.finish()
    grads.middle()
    back.finish()

    def project(i, total):
        lhs = jnp.concatenate([gbuf[4 * i + j] for j in range(4)], axis=1)
        return total + dot(lhs, owbuf[i], 1, 1)

    grad_normed = lax.fori_loop(0, CTX, project, jnp.zeros((TOK, TOK), F32))
    scaled = grad_normed * ng
    dots = dot_high(jnp.ones((8, TOK), F32), gated * scaled, 1, 1)
    gdot_b[v % 4] = dots[0:1]
    gdot_x.start(v % 4)

    @pl.loop(0, CTX)
    def _(i):
        lhs = jnp.concatenate([gbuf[4 * i + j] for j in range(4)], axis=1)
        osend[(i % 2) * 4 + i // 2] = dot(normed_t, lhs).astype(BF16)

    y_at, k_at = c // 2, c % 2
    side, c_p, c_m = y_at * 2 + 1 - k_at, ((y_at + 1) % 4) * 2 + k_at, ((y_at + 3) % 4) * 2 + k_at
    at_p, at_m, at_2 = k_at * 4 + (y_at + 1) % 4, k_at * 4 + (y_at + 3) % 4, k_at * 4 + (y_at + 2) % 4

    def os_copy(n, src, dst, to):
        return pltpu.make_async_remote_copy(
            src_ref=src, dst_ref=dst, send_sem=os_s.at[n], recv_sem=os_r.at[n], device_id={"ctx": to}, device_id_type=MESH
        )

    os_copies = (
        os_copy(0, osend.at[pl.ds((1 - k_at) * 4, 4)], obuf.at[pl.ds(0, 4)], side),
        os_copy(1, osend.at[at_2, top], orel.at[0], c_p),
        os_copy(2, osend.at[at_2, bottom], orel.at[1], c_m),
        os_copy(3, osend.at[at_p], obuf.at[4], c_p),
        os_copy(4, osend.at[at_m], obuf.at[5], c_m),
    )
    os_copies[0].start()
    gdot_x.got()
    gdot = wide(column(jnp.sum(gdot_b[...], axis=0)), TOK)
    grad_gated = ginv * scaled - gated * (ginv * ginv * ginv * gdot * (1.0 / (INNER // GROUPS)))
    gg_o[...] = (grad_gated * y * sig * (1.0 + zf * (1.0 - sig))).astype(BF16)
    gy = grad_gated * zf * sig
    gyb[...] = gy
    puts[4].start()
    gye = gy * grow_full
    h0 = vbuf[c, 0:128]
    dc = dot_both(gye, h0, 1, 1)
    vbuf[c, 0:128] = dot_right(cc, gye, 0, 0)
    vbuf[c, 128:STATE_ROWS] = jnp.zeros((STATE_ROWS - 128, TOK), F32)
    adjoints.start()

    ones8 = jnp.ones((8, TOK), F32)
    dcb = jnp.zeros((TOK, TOK), F32)
    rows_m, cols_m = [], []
    for h in range(4):
        if h == 2:
            os_copies[0].wait_recv()
            for j in (2, 1, 3):
                i = k_at * 4 + (y_at + 4 - j) % 4
                osend[i] = (osend[i].astype(F32) + obuf[(y_at + 4 - j) % 4].astype(F32)).astype(BF16)
                if j == 2:
                    os_copies[1].start()
                    os_copies[2].start()
            adjoints.middle()
        if h == 3:
            os_copies[1].wait_recv()
            osend[at_p, top] = (osend[at_p, top].astype(F32) + orel[0].astype(F32)).astype(BF16)
            os_copies[3].start()
            os_copies[2].wait_recv()
            osend[at_m, bottom] = (osend[at_m, bottom].astype(F32) + orel[1].astype(F32)).astype(BF16)
            os_copies[4].start()
        pair = h // 2
        gyp = gyb[:, pair * 128 : pair * 128 + 128]
        gym = jnp.where(low if h % 2 == 0 else jnp.logical_not(low), gyp, 0.0)
        e = es[h]
        s = cbb[...] * e
        ds = dot_left(gym, xb[:, pair * 128 : pair * 128 + 128], 1, 1)
        dcb = dcb + ds * e
        m = ds * s
        rows_m.append(dot_high(ones8, m, 1, 1)[0:1])
        cols_m.append(jnp.sum(m, axis=0, keepdims=True))
        part = dot_both(s, gym, 0, 0)
        if h % 2 == 0:
            held = part
        else:
            logits[:, pair * 128 : pair * 128 + 128] = held + part
    grads.end()
    adjoints.end()
    zero4 = jnp.zeros((4, TOK), F32)
    rows_m = jnp.concatenate(rows_m + [zero4], axis=0)
    cols_m = jnp.concatenate(cols_m + [zero4], axis=0)
    dc = dc + dot_left(dcb, b)
    db = dot_left(dcb, cc, 0, 0)
    r_rows = dot_high(sel, gy * cb_ch0[...], 1, 1)
    c_send[...] = dc.reshape(VOC, 8, 128).astype(BF16)
    c_x.start(v)
    c_got[v] = c_send[v]
    grads.finish()
    norm_x.got()
    acc[...] = jnp.zeros_like(acc)

    @pl.loop(0, CTX)
    def _(i):
        acc[...] += dot(ntbuf[i], gall[i])

    gh_o[...] = acc[...].astype(BF16)
    puts[0].start()
    adjoints.finish()

    def leave(j, h1):
        i = CTX - 1 - j
        new = ubuf[i, 128:129] * h1 + vbuf[i, 0:128]
        return jnp.where(i > c, new, h1)

    h1 = lax.fori_loop(0, CTX - 1, leave, jnp.zeros((128, TOK), F32))
    db = db + dot_both(tail_full * xf, h1, 1, 1)
    b_send[...] = db.reshape(VOC, 8, 128).astype(BF16)
    b_x.start(v)
    b_got[v] = b_send[v]
    bdh = dot_right(b, h1) * tail_full
    gx_o[...] = (logits[:, 0:TOK] + skip * gy + bdh).astype(BF16)
    puts[3].start()
    wq = dot_high(sel, bdh * xf, 1, 1)

    def again(j, h0):
        new = ubuf[j, 128:129] * h0 + ubuf[j, 0:128]
        return jnp.where(j < c, new, h0)

    h0 = lax.fori_loop(0, CTX - 1, again, jnp.zeros((128, TOK), F32))
    cross = jnp.sum(h0 * h1, axis=0, keepdims=True) * ubuf[c, 128:129]
    cross = dot_high(sel, jnp.broadcast_to(cross, (8, TOK)), 1, 1)[:, 0:1]
    gdt_o[...] = ((cols_m + wq) / dt)[0:4]
    da = rows_m - cols_m + r_rows - wq
    at_end = cross + jnp.sum(wq, axis=1, keepdims=True)
    gld_o[...] = (dot_high(da, (row_i >= col_i).astype(F32)) + at_end)[0:4]

    os_copies[3].wait_recv()
    os_copies[4].wait_recv()
    mine = k_at * 4 + y_at
    for j in range(4):
        cols = pl.ds(128 * j, 128)
        total = osend[mine, :, cols].astype(F32) + obuf[y_at, :, cols].astype(F32)
        gow_o[:, cols] = (total + obuf[4, :, cols].astype(F32) + obuf[5, :, cols].astype(F32)).astype(BF16)
    puts[2].start()
    c_x.got()
    b_x.got()
    for got, out in ((b_got, gb_o), (c_got, gc_o)):
        parts = []
        for g in range(GROUPS):
            four = [got[4 * g + j].astype(F32) for j in range(4)]
            parts.append((four[0] + four[1]) + (four[2] + four[3]))
        out[...] = jnp.concatenate(parts, axis=1).astype(BF16)

    for gather in (weights, outs_w, grads, states, adjoints):
        gather.drain()
    stream.drain()
    back.drain()
    for many in (lse_x, inner_x, gsum_x, gdot_x, norm_x, b_x, c_x, mean_x):
        many.drain()
    rs_wait(0, 0, rel_a, False)
    rs_wait(1, 0, rel_b, False)
    rs_wait(2, 0, from_m, False)
    rs_wait(3, 0, from_p, False)
    rs_wait(4, 0, rz.at[pl.ds(0, 7)], False)
    for copy in os_copies:
        copy.wait_send()
    for copy in puts:
        copy.wait()


def copy_kernel(*refs):
    n = len(refs) // 3
    ins, outs, bufs, (sin, sout) = refs[:n], refs[n : 2 * n], refs[2 * n : 3 * n], refs[3 * n :]
    loads = [pltpu.make_async_copy(ins[i], bufs[i], sin.at[i]) for i in range(n)]
    stores = [pltpu.make_async_copy(bufs[i], outs[i], sout.at[i]) for i in range(n)]
    for copy in loads:
        copy.start()
    for load, store in zip(loads, stores):
        load.wait()
        store.start()
    for store in stores:
        store.wait()


def hand_over(arrays):
    n = len(arrays)
    hbm = pl.BlockSpec(memory_space=pl.ANY)
    return pl.pallas_call(
        copy_kernel,
        out_shape=tuple(jax.ShapeDtypeStruct(a.shape, a.dtype) for a in arrays),
        in_specs=[hbm] * n,
        out_specs=(hbm,) * n,
        scratch_shapes=[pltpu.VMEM(a.shape, a.dtype) for a in arrays]
        + [pltpu.SemaphoreType.DMA((n,)), pltpu.SemaphoreType.DMA((n,))],
        name="hand_over",
    )(*arrays)


def shards(resid, gain, head_w, targets, out_w, norm_gain, xs, gate, b, c, dt, decay, skip):
    heads = skip.shape[0]
    args = (
        resid,
        gain.reshape(VOC, 1, 128),
        head_w,
        targets.reshape(1, TOK),
        out_w,
        norm_gain.reshape(1, TOK),
        xs,
        gate,
        b,
        c,
        dt,
        decay,
        skip,
    )
    vm = pl.BlockSpec(memory_space=pltpu.VMEM)
    hbm = pl.BlockSpec(memory_space=pl.ANY)
    shape = jax.ShapeDtypeStruct
    dma = pltpu.SemaphoreType.DMA
    scratch = [
        pltpu.VMEM((CTX, 512, 1024), BF16),
        pltpu.VMEM((CTX, TOK, 512), BF16),
        pltpu.VMEM((VOC, TOK, 128), BF16),
        pltpu.VMEM((CTX, TOK, 512), BF16),
        pltpu.VMEM((CTX, 512, TOK), BF16),
        pltpu.VMEM((CTX, 512, TOK), BF16),
        pltpu.VMEM((TOK, 1024), F32),
        pltpu.VMEM((CTX, TOK, 1024), BF16),
        pltpu.VMEM((VOC, TOK, 128), BF16),
        pltpu.VMEM((8, HALF, 128), BF16),
        pltpu.VMEM((8, HALF, 128), BF16),
        pltpu.VMEM((8, TOK, 128), BF16),
        pltpu.VMEM((8, TOK, 128), BF16),
        pltpu.VMEM((8, TOK, 128), BF16),
        pltpu.VMEM((VOC, TOK, 128), BF16),
        pltpu.VMEM((CTX, STATE_ROWS, TOK), F32),
        pltpu.VMEM((CTX, STATE_ROWS, TOK), F32),
        pltpu.VMEM((CTX, TOK, 512), BF16),
        pltpu.VMEM((CTX, TOK, 512), BF16),
        pltpu.VMEM((4, TOK, TOK), F32),
        pltpu.VMEM((512, 1024), F32),
        pltpu.VMEM((VOC, 1, TOK), F32),
        pltpu.VMEM((VOC, 2, TOK), F32),
        pltpu.VMEM((4, 1, TOK), F32),
        pltpu.VMEM((4, 1, TOK), F32),
        pltpu.VMEM((VOC, 1, 128), F32),
        pltpu.VMEM((VOC, 1, 128), F32),
        pltpu.VMEM((VOC, 8, 128), BF16),
        pltpu.VMEM((VOC, 8, 128), BF16),
        pltpu.VMEM((VOC, 8, 128), BF16),
        pltpu.VMEM((VOC, 8, 128), BF16),
        pltpu.VMEM((2, HALF, 512), BF16),
        pltpu.VMEM((TOK, TOK), BF16),
        pltpu.VMEM((TOK, TOK), BF16),
        pltpu.VMEM((TOK, 128), BF16),
        pltpu.VMEM((TOK, 128), BF16),
        pltpu.VMEM((512, 1024), BF16),
        pltpu.VMEM((TOK, 128), BF16),
        pltpu.VMEM((TOK, 512), BF16),
        pltpu.VMEM((TOK, TOK), BF16),
        pltpu.VMEM((TOK, TOK), BF16),
        pltpu.VMEM((TOK, 128), F32),
        pltpu.VMEM((TOK, TOK), F32),
        pltpu.VMEM((TOK, TOK), F32),
        pltpu.VMEM((TOK, TOK), F32),
        pltpu.VMEM((TOK, TOK), F32),
        dma((12,)),
        dma((11,)), dma((11,)), dma((11,)), dma((11,)), dma((11,)), dma((11,)), dma((11,)), dma((11,)), dma((11,)), dma((11,)),
        dma((5,)), dma((40,)), dma((5,)), dma((40,)),
        dma((5,)), dma((33,)),
        dma((8,)), dma((8,)),
        dma((5,)), dma((5,)),
    ]
    outs = pl.pallas_call(
        kernel,
        out_shape=(
            shape((512, 1024), BF16),
            shape((TOK, 128), BF16),
            shape((TOK, 512), BF16),
            shape((TOK, TOK), BF16),
            shape((TOK, TOK), BF16),
            shape((8, 1024), BF16),
            shape((8, 1024), BF16),
            shape((heads, TOK), F32),
            shape((heads, TOK), F32),
        ),
        in_specs=[hbm, vm, hbm, vm, hbm, vm, hbm, hbm, hbm, hbm, vm, vm] + [pl.BlockSpec(memory_space=pltpu.SMEM)],
        out_specs=(hbm,) * 5 + (vm,) * 4,
        scratch_shapes=scratch,
        compiler_params=pltpu.CompilerParams(
            collective_id=0, has_side_effects=True, vmem_limit_bytes=67043328
        ),
        name="step",
    )(*args)
    return hand_over(outs)


def solution(mesh):
    return jax.shard_map(
        shards,
        mesh=mesh,
        in_specs=(
            P("ctx", "vocab"),
            P(),
            P("ctx", "vocab"),
            P("ctx"),
            P("vocab", "ctx"),
            P("vocab"),
            P("ctx", "vocab"),
            P("ctx", "vocab"),
            P("ctx", None),
            P("ctx", None),
            P("vocab", "ctx"),
            P("vocab", "ctx"),
            P("vocab"),
        ),
        out_specs=(
            P("ctx", "vocab"),
            P("ctx", "vocab"),
            P("vocab", "ctx"),
            P("ctx", "vocab"),
            P("ctx", "vocab"),
            P(("ctx", "vocab"), None),
            P(("ctx", "vocab"), None),
            P("vocab", "ctx"),
            P("vocab", "ctx"),
        ),
        check_vma=False,
    )
```

```python
import functools

import jax
import jax.numpy as jnp
from jax import lax
from jax.experimental import pallas as pl
from jax.experimental.pallas import tpu as pltpu
from jax.sharding import PartitionSpec as P

MESH = pl.DeviceIdType.MESH
F32 = jnp.float32
BF16 = jnp.bfloat16
D = 4096
INNER = 8192
GROUPS = 8
EPS = 1e-05
CTX = 8
VOC = 32
TOK = 256
HIGH = lax.Precision.HIGHEST
STATE_ROWS = 160
HALF = TOK // 2


def dot(a, b, ca=1, cb=0):
    return lax.dot_general(a, b, (((ca,), (cb,)), ((), ())), preferred_element_type=F32)


def dot_high(a, b, ca=1, cb=0):
    return lax.dot_general(
        a, b, (((ca,), (cb,)), ((), ())), precision=HIGH, preferred_element_type=F32
    )


def halves(a):
    high = a.astype(BF16)
    return high, (a - high.astype(F32)).astype(BF16)


def dot_left(a, b, ca=1, cb=0):
    high, low = halves(a)
    return dot(high, b, ca, cb) + dot(low, b, ca, cb)


def dot_right(a, b, ca=1, cb=0):
    high, low = halves(b)
    return dot(a, high, ca, cb) + dot(a, low, ca, cb)


def dot_both(a, b, ca=1, cb=0):
    ah, al = halves(a)
    bh, bl = halves(b)
    return dot(ah, bh, ca, cb) + (dot(al, bh, ca, cb) + dot(ah, bl, ca, cb))


def column(row):
    return jnp.broadcast_to(row, (128, row.shape[1])).T


def row_of(col):
    return col.T[0:1]


def wide(col, lanes):
    return jnp.concatenate([col] * (lanes // 128), axis=1)


def send(src, dst, ssem, rsem, device):
    copy = pltpu.make_async_remote_copy(
        src_ref=src, dst_ref=dst, send_sem=ssem, recv_sem=rsem, device_id=device, device_id_type=MESH
    )
    copy.start()


class Ctx:
    def __init__(self, buf, ssem, rsem, c):
        y, k = c // 2, c % 2
        self.buf, self.s, self.r, self.c = buf, ssem, rsem, c
        at = lambda dy, kk: ((y + dy) % 4) * 2 + kk
        self.own, self.yp, self.ym, self.y2 = c, at(1, k), at(3, k), at(2, k)
        self.sib, self.syp, self.sym, self.sy2 = at(0, 1 - k), at(1, 1 - k), at(3, 1 - k), at(2, 1 - k)
        rows = buf.shape[1]
        self.top, self.bottom = pl.ds(0, rows // 2), pl.ds(rows // 2, rows // 2)

    def ref(self, block, part=None):
        return self.buf.at[block] if part is None else self.buf.at[block, part]

    def go(self, slot, block, to, part=None):
        ref = self.ref(block, part)
        send(ref, ref, self.s.at[slot], self.r.at[slot], {"ctx": to})

    def got(self, slot, block, part=None):
        ref = self.ref(block, part)
        pltpu.make_async_remote_copy(
            src_ref=ref, dst_ref=ref, send_sem=self.s.at[slot], recv_sem=self.r.at[slot],
            device_id={"ctx": self.sib}, device_id_type=MESH,
        ).wait_recv()

    def sent(self, slot, block, part=None):
        ref = self.ref(block, part)
        pltpu.make_async_remote_copy(
            src_ref=ref, dst_ref=ref, send_sem=self.s.at[slot], recv_sem=self.r.at[slot],
            device_id={"ctx": self.sib}, device_id_type=MESH,
        ).wait_send()

    def start(self):
        self.go(0, self.own, self.yp, self.top)
        self.go(1, self.own, self.ym, self.bottom)
        self.go(9, self.own, self.yp, self.bottom)
        self.go(10, self.own, self.ym, self.top)
        self.go(2, self.own, self.sib)

    def middle(self):
        self.got(0, self.ym, self.top)
        self.go(5, self.ym, self.yp, self.top)
        self.got(1, self.yp, self.bottom)
        self.go(6, self.yp, self.ym, self.bottom)
        self.got(9, self.ym, self.bottom)
        self.go(3, self.ym, self.sib)
        self.got(10, self.yp, self.top)
        self.go(4, self.yp, self.sib)

    def end(self):
        self.got(5, self.y2, self.top)
        self.go(7, self.y2, self.sib, self.top)
        self.got(6, self.y2, self.bottom)
        self.go(8, self.y2, self.sib, self.bottom)

    def finish(self):
        self.got(2, self.sib)
        self.got(3, self.sym)
        self.got(4, self.syp)
        self.last()

    def last(self):
        self.got(7, self.sy2, self.top)
        self.got(8, self.sy2, self.bottom)

    def drain(self):
        self.sent(0, self.own, self.top)
        self.sent(1, self.own, self.bottom)
        self.sent(9, self.own, self.bottom)
        self.sent(10, self.own, self.top)
        self.sent(2, self.own)
        self.sent(3, self.ym)
        self.sent(4, self.yp)
        self.sent(5, self.ym, self.top)
        self.sent(6, self.yp, self.bottom)
        self.sent(7, self.y2, self.top)
        self.sent(8, self.y2, self.bottom)


ORDER = (0, 1, 7, 2, 6, 3, 5, 4)
LAG = 3


class Voc:
    def __init__(self, buf, ssem, rsem, v):
        self.buf, self.s, self.r = buf, ssem, rsem
        self.x, self.z = v // 8, v % 8
        self.v = v
        self.xp, self.xm = (self.x + 1) % 4, (self.x + 3) % 4

    def wait(self, refs, sem_s, sem_r, receive):
        copy = pltpu.make_async_remote_copy(
            src_ref=refs, dst_ref=refs, send_sem=sem_s, recv_sem=sem_r,
            device_id={"vocab": self.xp * 8 + self.z}, device_id_type=MESH,
        )
        if receive:
            copy.wait_recv()
        else:
            copy.wait_send()

    def start(self):
        for d in (1, 7, 2, 6):
            ref = self.buf.at[self.v]
            send(ref, ref, self.s.at[0], self.r.at[d], {"vocab": self.x * 8 + (self.z + d) % 8})

    def forward(self, d):
        ref = self.buf.at[self.x * 8 + (self.z + 8 - d) % 8]
        if d:
            self.wait(ref, self.s.at[0], self.r.at[d], True)
        if d in (2, 3):
            send(ref, ref, self.s.at[0], self.r.at[d + 1], {"vocab": self.x * 8 + (self.z + 1) % 8})
        if d == 6:
            send(ref, ref, self.s.at[0], self.r.at[5], {"vocab": self.x * 8 + (self.z + 7) % 8})
        send(ref, ref, self.s.at[1], self.r.at[8 + d], {"vocab": self.xp * 8 + self.z})
        send(ref, ref, self.s.at[2], self.r.at[16 + d], {"vocab": self.xm * 8 + self.z})

    def pass_on(self, d):
        zz = (self.z + 8 - d) % 8
        block = self.xm * 8 + zz
        self.wait(self.buf.at[block], self.s.at[1], self.r.at[8 + d], True)
        ref = self.buf.at[block, pl.ds(0, HALF)]
        send(ref, ref, self.s.at[3], self.r.at[24 + d], {"vocab": self.xp * 8 + self.z})
        block = self.xp * 8 + zz
        self.wait(self.buf.at[block], self.s.at[2], self.r.at[16 + d], True)
        ref = self.buf.at[block, pl.ds(HALF, HALF)]
        send(ref, ref, self.s.at[4], self.r.at[32 + d], {"vocab": self.xm * 8 + self.z})

    def spread(self, first=0, stop=8):
        for n in range(first, stop):
            self.forward(ORDER[n])
            if n >= LAG:
                self.pass_on(ORDER[n - LAG])

    def relay(self):
        for n in range(8 - LAG, 8):
            self.pass_on(ORDER[n])

    def finish(self):
        for d in ORDER:
            block = ((self.x + 2) % 4) * 8 + (self.z + 8 - d) % 8
            self.wait(self.buf.at[block, pl.ds(0, HALF)], self.s.at[3], self.r.at[24 + d], True)
            self.wait(self.buf.at[block, pl.ds(HALF, HALF)], self.s.at[4], self.r.at[32 + d], True)

    def drain(self):
        self.wait(self.buf.at[pl.ds(0, 7)], self.s.at[0], self.r.at[0], False)
        self.wait(self.buf.at[pl.ds(0, 8)], self.s.at[1], self.r.at[0], False)
        self.wait(self.buf.at[pl.ds(0, 8)], self.s.at[2], self.r.at[0], False)
        self.wait(self.buf.at[pl.ds(0, 4)], self.s.at[3], self.r.at[0], False)
        self.wait(self.buf.at[pl.ds(0, 4)], self.s.at[4], self.r.at[0], False)


class Swap:
    def __init__(self, src, dst, rel, ssem, rsem, c):
        self.src, self.dst, self.rel, self.s, self.r, self.c = src, dst, rel, ssem, rsem, c
        y, self.k = c // 2, c % 2
        self.at = lambda dy, kk: ((y + dy) % 4) * 2 + kk
        self.top, self.bottom = pl.ds(0, TOK), pl.ds(TOK, TOK)

    def copy(self, slot, arrive, src, dst, to):
        return pltpu.make_async_remote_copy(
            src_ref=src, dst_ref=dst, send_sem=self.s.at[slot], recv_sem=self.r.at[arrive],
            device_id={"ctx": to}, device_id_type=MESH,
        )

    def sends(self):
        c, k, at = self.c, self.k, self.at
        first, second = [], []
        for kk in range(2):
            first.append((5 + kk, 5 + kk, self.src.at[at(2, kk), self.top], self.rel.at[kk], at(1, k)))
            first.append((7 + kk, 7 + kk, self.src.at[at(2, kk), self.bottom], self.rel.at[2 + kk], at(3, k)))
        for kk in range(2):
            first.append((kk, k, self.src.at[at(1, kk)], self.dst.at[c], at(1, kk)))
            first.append((2 + kk, 2 + k, self.src.at[at(3, kk)], self.dst.at[c], at(3, kk)))
            second.append((9 + kk, 9 + k, self.rel.at[kk], self.dst.at[at(3, k), self.top], at(1, kk)))
            second.append((11 + kk, 11 + k, self.rel.at[2 + kk], self.dst.at[at(1, k), self.bottom], at(3, kk)))
        first.append((4, 4, self.src.at[at(0, 1 - k)], self.dst.at[c], at(0, 1 - k)))
        return first, second

    def start(self):
        for args in self.sends()[0]:
            self.copy(*args).start()

    def got(self, arrive, ref):
        self.copy(0, arrive, ref, ref, self.at(1, self.k)).wait_recv()

    def forward(self):
        for i in range(4):
            self.got(5 + i, self.rel.at[i])
        for args in self.sends()[1]:
            self.copy(*args).start()

    def finish(self):
        for kk in range(2):
            self.got(kk, self.dst.at[self.at(3, kk)])
            self.got(2 + kk, self.dst.at[self.at(1, kk)])
            self.got(9 + kk, self.dst.at[self.at(2, kk), self.top])
            self.got(11 + kk, self.dst.at[self.at(2, kk), self.bottom])
        self.got(4, self.dst.at[self.at(0, 1 - self.k)])

    def drain(self):
        first, second = self.sends()
        for args in first + second:
            self.copy(*args).wait_send()


class Many:
    def __init__(self, axis, me, peer, count, src, dst, ssem, rsem):
        self.axis, self.me, self.peer, self.count = axis, me, peer, count
        self.src, self.dst, self.ssem, self.rsem = src, dst, ssem, rsem

    def start(self, slot):
        @pl.loop(1, self.count)
        def _(d):
            to = self.peer(d)
            send(self.src(to), self.dst.at[slot], self.ssem, self.rsem, {self.axis: to})

    def whole(self):
        refs = self.dst.at[pl.ds(0, self.count - 1)]
        return pltpu.make_async_remote_copy(
            src_ref=refs, dst_ref=refs, send_sem=self.ssem, recv_sem=self.rsem,
            device_id={self.axis: self.peer(1)}, device_id_type=MESH,
        )

    def got(self):
        self.whole().wait_recv()

    def drain(self):
        self.whole().wait_send()


def kernel(*refs):
    (resid, gain, head_w, target, out_w, norm_gain, xs, gate, b_in, c_in, dt_in, decay_in, skip_in) = refs[:13]
    (gh_h, gr_h, gow_h, gx_h, gg_h, gb_o, gc_o, gdt_o, gld_o) = refs[13:22]
    (wbuf, owbuf, sbuf, nbuf, ntsend, ntbuf, logits, gall, pbuf, rel_a, rel_b, from_m, from_p, rz, gbuf,
     ubuf, vbuf, osend, obuf, es, acc, lse_b, inner_b, gsum_b, gdot_b, mean_s, mean_b, b_send, b_got, c_send, c_got, orel, nrel, xs_v, gate_v, b_v, c_v, gh_o, gr_o, gow_o, gx_o, gg_o, mcol, ycur, cbb, cb_ch0, gyb,
     lsem, ws, wr, ows, owr, gs, gr, us, ur, vs, vr, s1s, s1r, s2s, s2r, rs_s, rs_r, ms, mr, os_s, os_r, nt_s, nt_r) = refs[22:]
    c = lax.axis_index("ctx")
    v = lax.axis_index("vocab")
    x, z = v // 8, v % 8
    xp, xm, x2 = (x + 1) % 4, (x + 3) % 4, (x + 2) % 4

    lanes = pl.ds(pl.multiple_of((v // 4) * 128, 128), 128)
    barrier = pltpu.get_barrier_semaphore()

    @pl.loop(1, VOC)
    def _(d):
        pl.semaphore_signal(barrier, inc=1, device_id={"vocab": (v + d) % VOC}, device_id_type=MESH)

    @pl.loop(1, CTX)
    def _(d):
        pl.semaphore_signal(barrier, inc=1, device_id={"ctx": (c + d) % CTX}, device_id_type=MESH)

    local = [
        pltpu.make_async_copy(resid, sbuf.at[v], lsem.at[0]),
        pltpu.make_async_copy(head_w, wbuf.at[c], lsem.at[1]),
        pltpu.make_async_copy(out_w, owbuf.at[c], lsem.at[2]),
        pltpu.make_async_copy(xs, xs_v, lsem.at[3]),
        pltpu.make_async_copy(gate, gate_v, lsem.at[4]),
        pltpu.make_async_copy(b_in.at[:, lanes], b_v, lsem.at[5]),
        pltpu.make_async_copy(c_in.at[:, lanes], c_v, lsem.at[6]),
    ]
    for copy in local:
        copy.start()
    for copy in local[:2]:
        copy.wait()
    pl.semaphore_wait(barrier, VOC + CTX - 2)

    weights = Ctx(wbuf, ws, wr, c)
    outs_w = Ctx(owbuf, ows, owr, c)
    grads = Ctx(gall, gs, gr, c)
    states = Ctx(ubuf, us, ur, c)
    adjoints = Ctx(vbuf, vs, vr, c)
    stream = Voc(sbuf, s1s, s1r, v)
    back = Voc(gbuf, s2s, s2r, v)
    over_v = lambda d: (v + d) % VOC
    quarter = (v // 4) * 4
    over_g = lambda d: quarter + (v % 4 + d) % 4
    lse_x = Many("vocab", v, over_v, VOC, lambda to: lse_b.at[v], lse_b, ms.at[0], mr.at[0])
    inner_x = Many("vocab", v, over_v, VOC, lambda to: inner_b.at[v], inner_b, ms.at[1], mr.at[1])
    gsum_x = Many("vocab", v, over_g, 4, lambda to: gsum_b.at[v % 4], gsum_b, ms.at[2], mr.at[2])
    gdot_x = Many("vocab", v, over_g, 4, lambda to: gdot_b.at[v % 4], gdot_b, ms.at[3], mr.at[3])
    norms = Swap(ntsend, ntbuf, nrel, nt_s, nt_r, c)
    b_x = Many("vocab", v, over_v, VOC, lambda to: b_send.at[to], b_got, ms.at[6], mr.at[6])
    c_x = Many("vocab", v, over_v, VOC, lambda to: c_send.at[to], c_got, ms.at[5], mr.at[5])
    mean_x = Many("vocab", v, over_v, VOC, lambda to: mean_s.at[to], mean_b, ms.at[7], mr.at[7])

    puts = [
        pltpu.make_async_copy(src, dst, lsem.at[7 + n])
        for n, (src, dst) in enumerate(
            ((gh_o, gh_h), (gr_o, gr_h), (gow_o, gow_h), (gx_o, gx_h), (gg_o, gg_h))
        )
    ]
    stream.start()
    weights.start()
    stream.spread()

    for copy in local[2:]:
        copy.wait()
    b = b_v[...]
    cc = c_v[...]
    xb = xs_v[...]
    xf = xb.astype(F32)
    row_i = lax.broadcasted_iota(jnp.int32, (TOK, TOK), 0)
    col_i = lax.broadcasted_iota(jnp.int32, (TOK, TOK), 1)
    upper = (row_i <= col_i).astype(F32)
    head_of = lax.broadcasted_iota(jnp.int32, (8, TOK), 1) // 64
    sel = (head_of == lax.broadcasted_iota(jnp.int32, (8, TOK), 0)).astype(F32)
    dt = jnp.concatenate([dt_in[...], jnp.ones((4, TOK), F32)], axis=0)
    decay = jnp.concatenate([decay_in[...], jnp.zeros((4, TOK), F32)], axis=0)
    a = dot_high(decay, upper)
    last = a[:, TOK - 1 :]
    tail = jnp.exp(last - a) * dt
    a_cols = jnp.concatenate([a] * 16, axis=0).T
    cbb[...] = dot(cc, b, 1, 1)
    skip = jnp.zeros((1, TOK), F32)
    for h in range(4):
        skip = skip + sel[h : h + 1] * skip_in[h]
    low = lax.broadcasted_iota(jnp.int32, (TOK, 128), 1) < 64
    for pair in range(2):
        outs = []
        for h in (2 * pair, 2 * pair + 1):
            gap = a_cols[:, h : h + 1] - a[h : h + 1]
            e = jnp.exp(jnp.where(row_i >= col_i, gap, -1e30)) * dt[h : h + 1]
            es[h] = e
            outs.append(dot_left(cbb[...] * e, xb[:, pair * 128 : pair * 128 + 128]))
        ycur[:, pair * 128 : pair * 128 + 128] = jnp.where(low, outs[0], outs[1])
    tail_full = dot_high(tail, sel, 0, 0)
    grow_full = dot_high(jnp.exp(a), sel, 0, 0)
    ubuf[c, 0:128] = dot_right(b, tail_full * xf, 0, 0)
    whole = dot_high(jnp.broadcast_to(jnp.exp(last), (8, 128)), sel, 0, 0)
    ubuf[c, 128:STATE_ROWS] = whole[0 : STATE_ROWS - 128]

    stream.relay()
    weights.middle()
    stream.finish()

    def square(i, total):
        block = sbuf[i].astype(F32)
        return total + block * block

    total = lax.fori_loop(0, VOC, square, jnp.zeros((TOK, 128), F32))
    inv = lax.rsqrt(jnp.sum(total, axis=1, keepdims=True) * (1.0 / D) + EPS)
    inv = jnp.broadcast_to(inv, (TOK, 128))

    @pl.loop(0, CTX)
    def _(i):
        parts = []
        for j in range(4):
            parts.append((sbuf[4 * i + j].astype(F32) * inv * gain[4 * i + j]).astype(BF16))
        block = jnp.concatenate(parts, axis=1)
        nbuf[i] = block
        ntsend[i] = block.T

    ntbuf[c] = ntsend[c]

    def logit(i, first=False):
        part = dot(nbuf[i], wbuf[i])
        if first:
            logits[...] = part
        else:
            logits[...] += part

    logit(weights.own, True)
    weights.got(2, weights.sib)
    logit(weights.sib)
    logit(weights.ym)
    logit(weights.yp)
    weights.end()
    logit(weights.y2)
    weights.got(3, weights.sym)
    logit(weights.sym)
    weights.got(4, weights.syp)
    logit(weights.syp)
    weights.last()
    logit(weights.sy2)

    states.start()
    outs_w.start()

    @pl.loop(0, 4)
    def _(i):
        rows = pl.ds(pl.multiple_of(i * 64, 64), 64)
        part = logits[rows, :]
        most = jnp.max(part, axis=1, keepdims=True)
        value = most + jnp.log(jnp.sum(jnp.exp(part - most), axis=1, keepdims=True))
        mcol[rows, :] = jnp.broadcast_to(value, (64, 128))

    lse_b[v] = row_of(mcol[...])
    lse_x.start(v)
    target_col = column(target[...].astype(F32))
    lse_x.got()
    every = lse_b[...]
    most = jnp.max(every, axis=0)
    log_norm = most + jnp.log(jnp.sum(jnp.exp(every - most[None]), axis=0))
    mcol[...] = column(log_norm)
    cb_ch0[:, 0:128] = target_col

    base = (v * 1024).astype(F32)
    ids = lax.broadcasted_iota(jnp.int32, (64, 1024), 1).astype(F32) + base

    @pl.loop(0, 4)
    def _(i):
        rows = pl.ds(pl.multiple_of(i * 64, 64), 64)
        part = logits[rows, :]
        hit = jnp.where(wide(cb_ch0[rows, 0:128], 1024) == ids, 1.0, 0.0)
        g = (jnp.exp(part - wide(mcol[rows, :], 1024)) - hit).astype(BF16)
        gall[c, rows, :] = g
        value = jnp.sum(g.astype(F32) * part, axis=1, keepdims=True)
        mcol[rows, :] = jnp.broadcast_to(value, (64, 128))
        value = jnp.sum(g.astype(F32), axis=1, keepdims=True)
        cb_ch0[rows, 128:256] = jnp.broadcast_to(value, (64, 128))

    inner_b[v, 0:1] = row_of(mcol[...])
    inner_b[v, 1:2] = row_of(cb_ch0[:, 128:256])
    inner_x.start(v)

    top, bottom = pl.ds(0, HALF), pl.ds(HALF, HALF)

    weigh = jnp.concatenate([gall[c], jnp.full((16, 1024), 2.0**-10, BF16)], axis=0)
    sums_g = cb_ch0[:, 128:256]

    def partial(i):
        part = dot(weigh, wbuf[i], 1, 1)
        for j in range(4):
            mean = part[TOK : TOK + 1, j * 128 : j * 128 + 128]
            mean_s[4 * i + j] = mean
            pbuf[4 * i + j] = (part[0:TOK, j * 128 : j * 128 + 128] - sums_g * mean).astype(BF16)

    to_p, to_m = {"vocab": xp * 8 + z}, {"vocab": xm * 8 + z}

    def rs_send(kind, n, src, dst, to):
        send(src, dst, rs_s.at[kind], rs_r.at[8 * kind + n], to)

    def rs_wait(kind, n, ref, receive=True):
        copy = pltpu.make_async_remote_copy(
            src_ref=ref, dst_ref=ref, send_sem=rs_s.at[kind], recv_sem=rs_r.at[8 * kind + n],
            device_id=to_p, device_id_type=MESH,
        )
        if receive:
            copy.wait_recv()
        else:
            copy.wait_send()

    far, near = 1 - z // 4, z // 4
    serve = [4 * far + (z % 4 + 1 + j) % 4 for j in range(4)] + [4 * near + (z % 4 + 1 + j) % 4 for j in range(4)]
    def first_relays(ns):
        for n in ns:
            rs_send(0, n, pbuf.at[x2 * 8 + serve[n], top], rel_a.at[n], to_p)
            rs_send(1, n, pbuf.at[x2 * 8 + serve[n], bottom], rel_b.at[n], to_m)

    def relayed(n):
        rs_wait(0, n, rel_a.at[n])
        i = xp * 8 + serve[n]
        pbuf[i, 0:HALF] = (pbuf[i, 0:HALF].astype(F32) + rel_a[n].astype(F32)).astype(BF16)
        rs_send(2, n, pbuf.at[i], from_m.at[n], to_p)
        rs_wait(1, n, rel_b.at[n])
        i = xm * 8 + serve[n]
        pbuf[i, HALF:TOK] = (pbuf[i, HALF:TOK].astype(F32) + rel_b[n].astype(F32)).astype(BF16)
        rs_send(3, n, pbuf.at[i], from_p.at[n], to_m)

    def collect(n):
        rs_wait(2, n, from_m.at[n])
        rs_wait(3, n, from_p.at[n])
        i = x * 8 + serve[n]
        total = pbuf[i].astype(F32) + from_m[n].astype(F32) + from_p[n].astype(F32)
        pbuf[i] = total.astype(BF16)
        if n < 7:
            send(pbuf.at[i], rz.at[z], rs_s.at[4], rs_r.at[32], {"vocab": i})

    partial(2 * x2 + far)
    first_relays(range(4))
    partial(2 * xp + far)
    partial(2 * xm + far)
    for n in range(4):
        relayed(n)
    partial(2 * x2 + near)
    first_relays(range(4, 8))
    grads.start()
    partial(2 * x + far)
    partial(2 * xp + near)
    partial(2 * xm + near)
    partial(2 * x + near)
    mean_b[v] = mean_s[v]
    mean_x.start(v)
    states.middle()
    outs_w.middle()
    norms.start()

    for n in range(4):
        collect(n)
    for n in range(4, 8):
        relayed(n)
    for n in range(4, 8):
        collect(n)
    rz[z] = pbuf[v]

    inner_x.got()
    inner = column(jnp.sum(inner_b[...], axis=0)[0:1])
    mean_x.got()
    extra = dot_high(inner_b[:, 1, :], mean_b[:, 0, :], 0, 0)
    resid_f = sbuf[v].astype(F32)
    less = resid_f * (inv * inv * inner * (1.0 / D))
    rs_wait(4, 0, rz.at[pl.ds(0, 7)])
    total = extra
    for j in range(8):
        total = total + rz[j].astype(F32)
    mine = (inv * (total * gain[v]) - less).astype(BF16)
    gr_o[...] = mine
    puts[1].start()
    gbuf[v] = mine
    back.start()
    back.spread(0, 5)
    states.end()
    outs_w.end()
    back.spread(5, 8)
    norms.forward()
    back.relay()
    states.finish()

    def enter(j, h0):
        new = ubuf[j, 128:129] * h0 + ubuf[j, 0:128]
        return jnp.where(j < c, new, h0)

    h0 = lax.fori_loop(0, CTX - 1, enter, jnp.zeros((128, TOK), F32))
    vbuf[c, 0:128] = h0
    ch0 = dot_right(cc, h0) * grow_full
    cb_ch0[...] = ch0
    y = ycur[...] + ch0 + skip * xf
    ycur[...] = y
    zf = gate_v[...].astype(F32)
    sig = 1.0 / (1.0 + jnp.exp(-zf))
    gated = y * zf * sig
    squares = dot_high(jnp.ones((8, TOK), F32), gated * gated, 1, 1)
    gsum_b[v % 4] = squares[0:1]
    gsum_x.start(v % 4)

    ng = norm_gain[...]
    grads.middle()
    outs_w.finish()
    back.finish()

    def project(i, total):
        lhs = jnp.concatenate([gbuf[4 * i + j] for j in range(4)], axis=1)
        return total + dot(lhs, owbuf[i], 1, 1)

    grad_normed = lax.fori_loop(0, CTX, project, jnp.zeros((TOK, TOK), F32))
    scaled = grad_normed * ng
    dots = dot_high(jnp.ones((8, TOK), F32), gated * scaled, 1, 1)
    gdot_b[v % 4] = dots[0:1]
    gdot_x.start(v % 4)
    gsum_x.got()
    sums = jnp.sum(gsum_b[...], axis=0)
    ginv = column(lax.rsqrt(sums * (1.0 / (INNER // GROUPS)) + EPS))
    ginv = wide(ginv, TOK)
    normed_t = (gated * ginv * ng).astype(BF16).T

    @pl.loop(0, CTX)
    def _(i):
        lhs = jnp.concatenate([gbuf[4 * i + j] for j in range(4)], axis=1)
        osend[(i % 2) * 4 + i // 2] = dot(normed_t, lhs).astype(BF16)

    y_at, k_at = c // 2, c % 2
    side, c_p, c_m = y_at * 2 + 1 - k_at, ((y_at + 1) % 4) * 2 + k_at, ((y_at + 3) % 4) * 2 + k_at
    at_p, at_m, at_2 = k_at * 4 + (y_at + 1) % 4, k_at * 4 + (y_at + 3) % 4, k_at * 4 + (y_at + 2) % 4

    def os_copy(n, src, dst, to):
        return pltpu.make_async_remote_copy(
            src_ref=src, dst_ref=dst, send_sem=os_s.at[n], recv_sem=os_r.at[n], device_id={"ctx": to}, device_id_type=MESH
        )

    os_copies = (
        os_copy(0, osend.at[pl.ds((1 - k_at) * 4, 4)], obuf.at[pl.ds(0, 4)], side),
        os_copy(1, osend.at[at_2, top], orel.at[0], c_p),
        os_copy(2, osend.at[at_2, bottom], orel.at[1], c_m),
        os_copy(3, osend.at[at_p], obuf.at[4], c_p),
        os_copy(4, osend.at[at_m], obuf.at[5], c_m),
    )
    os_copies[0].start()
    gdot_x.got()
    gdot = wide(column(jnp.sum(gdot_b[...], axis=0)), TOK)
    grad_gated = ginv * scaled - gated * (ginv * ginv * ginv * gdot * (1.0 / (INNER // GROUPS)))
    gg_o[...] = (grad_gated * y * sig * (1.0 + zf * (1.0 - sig))).astype(BF16)
    gy = grad_gated * zf * sig
    gyb[...] = gy
    puts[4].start()
    gye = gy * grow_full
    h0 = vbuf[c, 0:128]
    dc = dot_both(gye, h0, 1, 1)
    vbuf[c, 0:128] = dot_right(cc, gye, 0, 0)
    vbuf[c, 128:STATE_ROWS] = jnp.zeros((STATE_ROWS - 128, TOK), F32)
    adjoints.start()

    ones8 = jnp.ones((8, TOK), F32)
    dcb = jnp.zeros((TOK, TOK), F32)
    rows_m, cols_m = [], []
    for h in range(4):
        if h == 2:
            os_copies[0].wait_recv()
            for j in (2, 1, 3):
                i = k_at * 4 + (y_at + 4 - j) % 4
                osend[i] = (osend[i].astype(F32) + obuf[(y_at + 4 - j) % 4].astype(F32)).astype(BF16)
                if j == 2:
                    os_copies[1].start()
                    os_copies[2].start()
        pair = h // 2
        gyp = gyb[:, pair * 128 : pair * 128 + 128]
        gym = jnp.where(low if h % 2 == 0 else jnp.logical_not(low), gyp, 0.0)
        e = es[h]
        s = cbb[...] * e
        ds = dot_left(gym, xb[:, pair * 128 : pair * 128 + 128], 1, 1)
        dcb = dcb + ds * e
        m = ds * s
        rows_m.append(dot_high(ones8, m, 1, 1)[0:1])
        cols_m.append(jnp.sum(m, axis=0, keepdims=True))
        part = dot_both(s, gym, 0, 0)
        if h % 2 == 0:
            held = part
        else:
            logits[:, pair * 128 : pair * 128 + 128] = held + part
    adjoints.middle()
    os_copies[1].wait_recv()
    osend[at_p, top] = (osend[at_p, top].astype(F32) + orel[0].astype(F32)).astype(BF16)
    os_copies[3].start()
    os_copies[2].wait_recv()
    osend[at_m, bottom] = (osend[at_m, bottom].astype(F32) + orel[1].astype(F32)).astype(BF16)
    os_copies[4].start()
    zero4 = jnp.zeros((4, TOK), F32)
    rows_m = jnp.concatenate(rows_m + [zero4], axis=0)
    cols_m = jnp.concatenate(cols_m + [zero4], axis=0)
    dc = dc + dot_left(dcb, b)
    db = dot_left(dcb, cc, 0, 0)
    r_rows = dot_high(sel, gy * cb_ch0[...], 1, 1)
    c_send[...] = dc.reshape(VOC, 8, 128).astype(BF16)
    c_x.start(v)
    c_got[v] = c_send[v]
    adjoints.end()
    grads.end()
    adjoints.finish()

    def leave(j, h1):
        i = CTX - 1 - j
        new = ubuf[i, 128:129] * h1 + vbuf[i, 0:128]
        return jnp.where(i > c, new, h1)

    h1 = lax.fori_loop(0, CTX - 1, leave, jnp.zeros((128, TOK), F32))
    db = db + dot_both(tail_full * xf, h1, 1, 1)
    b_send[...] = db.reshape(VOC, 8, 128).astype(BF16)
    b_x.start(v)
    b_got[v] = b_send[v]
    bdh = dot_right(b, h1) * tail_full
    gx_o[...] = (logits[:, 0:TOK] + skip * gy + bdh).astype(BF16)
    puts[3].start()
    wq = dot_high(sel, bdh * xf, 1, 1)

    def again(j, h0):
        new = ubuf[j, 128:129] * h0 + ubuf[j, 0:128]
        return jnp.where(j < c, new, h0)

    h0 = lax.fori_loop(0, CTX - 1, again, jnp.zeros((128, TOK), F32))
    cross = jnp.sum(h0 * h1, axis=0, keepdims=True) * ubuf[c, 128:129]
    cross = dot_high(sel, jnp.broadcast_to(cross, (8, TOK)), 1, 1)[:, 0:1]
    gdt_o[...] = ((cols_m + wq) / dt)[0:4]
    da = rows_m - cols_m + r_rows - wq
    at_end = cross + jnp.sum(wq, axis=1, keepdims=True)
    gld_o[...] = (dot_high(da, (row_i >= col_i).astype(F32)) + at_end)[0:4]

    grads.finish()
    norms.finish()
    acc[...] = jnp.zeros_like(acc)

    @pl.loop(0, CTX)
    def _(i):
        acc[...] += dot(ntbuf[i], gall[i])

    gh_o[...] = acc[...].astype(BF16)
    puts[0].start()

    os_copies[3].wait_recv()
    os_copies[4].wait_recv()
    mine = k_at * 4 + y_at
    for j in range(4):
        cols = pl.ds(128 * j, 128)
        total = osend[mine, :, cols].astype(F32) + obuf[y_at, :, cols].astype(F32)
        gow_o[:, cols] = (total + obuf[4, :, cols].astype(F32) + obuf[5, :, cols].astype(F32)).astype(BF16)
    puts[2].start()
    c_x.got()
    b_x.got()
    for got, out in ((b_got, gb_o), (c_got, gc_o)):
        parts = []
        for g in range(GROUPS):
            four = [got[4 * g + j].astype(F32) for j in range(4)]
            parts.append((four[0] + four[1]) + (four[2] + four[3]))
        out[...] = jnp.concatenate(parts, axis=1).astype(BF16)

    for gather in (weights, outs_w, grads, states, adjoints):
        gather.drain()
    norms.drain()
    stream.drain()
    back.drain()
    for many in (lse_x, inner_x, gsum_x, gdot_x, b_x, c_x, mean_x):
        many.drain()
    rs_wait(0, 0, rel_a, False)
    rs_wait(1, 0, rel_b, False)
    rs_wait(2, 0, from_m, False)
    rs_wait(3, 0, from_p, False)
    rs_wait(4, 0, rz.at[pl.ds(0, 7)], False)
    for copy in os_copies:
        copy.wait_send()
    for copy in puts:
        copy.wait()


def copy_kernel(*refs):
    n = len(refs) // 3
    ins, outs, bufs, (sin, sout) = refs[:n], refs[n : 2 * n], refs[2 * n : 3 * n], refs[3 * n :]
    loads = [pltpu.make_async_copy(ins[i], bufs[i], sin.at[i]) for i in range(n)]
    stores = [pltpu.make_async_copy(bufs[i], outs[i], sout.at[i]) for i in range(n)]
    for copy in loads:
        copy.start()
    for load, store in zip(loads, stores):
        load.wait()
        store.start()
    for store in stores:
        store.wait()


def hand_over(arrays):
    n = len(arrays)
    hbm = pl.BlockSpec(memory_space=pl.ANY)
    return pl.pallas_call(
        copy_kernel,
        out_shape=tuple(jax.ShapeDtypeStruct(a.shape, a.dtype) for a in arrays),
        in_specs=[hbm] * n,
        out_specs=(hbm,) * n,
        scratch_shapes=[pltpu.VMEM(a.shape, a.dtype) for a in arrays]
        + [pltpu.SemaphoreType.DMA((n,)), pltpu.SemaphoreType.DMA((n,))],
        name="hand_over",
    )(*arrays)


def shards(resid, gain, head_w, targets, out_w, norm_gain, xs, gate, b, c, dt, decay, skip):
    heads = skip.shape[0]
    args = (
        resid,
        gain.reshape(VOC, 1, 128),
        head_w,
        targets.reshape(1, TOK),
        out_w,
        norm_gain.reshape(1, TOK),
        xs,
        gate,
        b,
        c,
        dt,
        decay,
        skip,
    )
    vm = pl.BlockSpec(memory_space=pltpu.VMEM)
    hbm = pl.BlockSpec(memory_space=pl.ANY)
    shape = jax.ShapeDtypeStruct
    dma = pltpu.SemaphoreType.DMA
    scratch = [
        pltpu.VMEM((CTX, 512, 1024), BF16),
        pltpu.VMEM((CTX, TOK, 512), BF16),
        pltpu.VMEM((VOC, TOK, 128), BF16),
        pltpu.VMEM((CTX, TOK, 512), BF16),
        pltpu.VMEM((CTX, 512, TOK), BF16),
        pltpu.VMEM((CTX, 512, TOK), BF16),
        pltpu.VMEM((TOK, 1024), F32),
        pltpu.VMEM((CTX, TOK, 1024), BF16),
        pltpu.VMEM((VOC, TOK, 128), BF16),
        pltpu.VMEM((8, HALF, 128), BF16),
        pltpu.VMEM((8, HALF, 128), BF16),
        pltpu.VMEM((8, TOK, 128), BF16),
        pltpu.VMEM((8, TOK, 128), BF16),
        pltpu.VMEM((8, TOK, 128), BF16),
        pltpu.VMEM((VOC, TOK, 128), BF16),
        pltpu.VMEM((CTX, STATE_ROWS, TOK), F32),
        pltpu.VMEM((CTX, STATE_ROWS, TOK), F32),
        pltpu.VMEM((CTX, TOK, 512), BF16),
        pltpu.VMEM((CTX, TOK, 512), BF16),
        pltpu.VMEM((4, TOK, TOK), F32),
        pltpu.VMEM((512, 1024), F32),
        pltpu.VMEM((VOC, 1, TOK), F32),
        pltpu.VMEM((VOC, 2, TOK), F32),
        pltpu.VMEM((4, 1, TOK), F32),
        pltpu.VMEM((4, 1, TOK), F32),
        pltpu.VMEM((VOC, 1, 128), F32),
        pltpu.VMEM((VOC, 1, 128), F32),
        pltpu.VMEM((VOC, 8, 128), BF16),
        pltpu.VMEM((VOC, 8, 128), BF16),
        pltpu.VMEM((VOC, 8, 128), BF16),
        pltpu.VMEM((VOC, 8, 128), BF16),
        pltpu.VMEM((2, HALF, 512), BF16),
        pltpu.VMEM((4, TOK, TOK), BF16),
        pltpu.VMEM((TOK, TOK), BF16),
        pltpu.VMEM((TOK, TOK), BF16),
        pltpu.VMEM((TOK, 128), BF16),
        pltpu.VMEM((TOK, 128), BF16),
        pltpu.VMEM((512, 1024), BF16),
        pltpu.VMEM((TOK, 128), BF16),
        pltpu.VMEM((TOK, 512), BF16),
        pltpu.VMEM((TOK, TOK), BF16),
        pltpu.VMEM((TOK, TOK), BF16),
        pltpu.VMEM((TOK, 128), F32),
        pltpu.VMEM((TOK, TOK), F32),
        pltpu.VMEM((TOK, TOK), F32),
        pltpu.VMEM((TOK, TOK), F32),
        pltpu.VMEM((TOK, TOK), F32),
        dma((12,)),
        dma((11,)), dma((11,)), dma((11,)), dma((11,)), dma((11,)), dma((11,)), dma((11,)), dma((11,)), dma((11,)), dma((11,)),
        dma((5,)), dma((40,)), dma((5,)), dma((40,)),
        dma((5,)), dma((33,)),
        dma((8,)), dma((8,)),
        dma((5,)), dma((5,)),
        dma((13,)), dma((13,)),
    ]
    outs = pl.pallas_call(
        kernel,
        out_shape=(
            shape((512, 1024), BF16),
            shape((TOK, 128), BF16),
            shape((TOK, 512), BF16),
            shape((TOK, TOK), BF16),
            shape((TOK, TOK), BF16),
            shape((8, 1024), BF16),
            shape((8, 1024), BF16),
            shape((heads, TOK), F32),
            shape((heads, TOK), F32),
        ),
        in_specs=[hbm, vm, hbm, vm, hbm, vm, hbm, hbm, hbm, hbm, vm, vm] + [pl.BlockSpec(memory_space=pltpu.SMEM)],
        out_specs=(hbm,) * 5 + (vm,) * 4,
        scratch_shapes=scratch,
        compiler_params=pltpu.CompilerParams(
            collective_id=0, has_side_effects=True, vmem_limit_bytes=67043328
        ),
        name="step",
    )(*args)
    return hand_over(outs)


def solution(mesh):
    return jax.shard_map(
        shards,
        mesh=mesh,
        in_specs=(
            P("ctx", "vocab"),
            P(),
            P("ctx", "vocab"),
            P("ctx"),
            P("vocab", "ctx"),
            P("vocab"),
            P("ctx", "vocab"),
            P("ctx", "vocab"),
            P("ctx", None),
            P("ctx", None),
            P("vocab", "ctx"),
            P("vocab", "ctx"),
            P("vocab"),
        ),
        out_specs=(
            P("ctx", "vocab"),
            P("ctx", "vocab"),
            P("vocab", "ctx"),
            P("ctx", "vocab"),
            P("ctx", "vocab"),
            P(("ctx", "vocab"), None),
            P(("ctx", "vocab"), None),
            P("vocab", "ctx"),
            P("vocab", "ctx"),
        ),
        check_vma=False,
    )
```

```python
import functools

import jax
import jax.numpy as jnp
from jax import lax
from jax.experimental import pallas as pl
from jax.experimental.pallas import tpu as pltpu
from jax.sharding import PartitionSpec as P

MESH = pl.DeviceIdType.MESH
F32 = jnp.float32
BF16 = jnp.bfloat16
D = 4096
INNER = 8192
GROUPS = 8
EPS = 1e-05
CTX = 8
VOC = 32
TOK = 256
HIGH = lax.Precision.HIGHEST
STATE_ROWS = 144
HALF = TOK // 2


def dot(a, b, ca=1, cb=0):
    return lax.dot_general(a, b, (((ca,), (cb,)), ((), ())), preferred_element_type=F32)


def dot_high(a, b, ca=1, cb=0):
    return lax.dot_general(
        a, b, (((ca,), (cb,)), ((), ())), precision=HIGH, preferred_element_type=F32
    )


def halves(a):
    high = a.astype(BF16)
    return high, (a - high.astype(F32)).astype(BF16)


def dot_left(a, b, ca=1, cb=0):
    high, low = halves(a)
    return dot(high, b, ca, cb) + dot(low, b, ca, cb)


def dot_right(a, b, ca=1, cb=0):
    high, low = halves(b)
    return dot(a, high, ca, cb) + dot(a, low, ca, cb)


def dot_both(a, b, ca=1, cb=0):
    ah, al = halves(a)
    bh, bl = halves(b)
    return dot(ah, bh, ca, cb) + (dot(al, bh, ca, cb) + dot(ah, bl, ca, cb))


def column(row):
    return jnp.broadcast_to(row, (128, row.shape[1])).T


def row_of(col):
    return col.T[0:1]


def wide(col, lanes):
    return jnp.concatenate([col] * (lanes // 128), axis=1)


def send(src, dst, ssem, rsem, device):
    copy = pltpu.make_async_remote_copy(
        src_ref=src, dst_ref=dst, send_sem=ssem, recv_sem=rsem, device_id=device, device_id_type=MESH
    )
    copy.start()


class Ctx:
    def __init__(self, buf, ssem, rsem, c):
        y, k = c // 2, c % 2
        self.buf, self.s, self.r, self.c = buf, ssem, rsem, c
        at = lambda dy, kk: ((y + dy) % 4) * 2 + kk
        self.own, self.yp, self.ym, self.y2 = c, at(1, k), at(3, k), at(2, k)
        self.sib, self.syp, self.sym, self.sy2 = at(0, 1 - k), at(1, 1 - k), at(3, 1 - k), at(2, 1 - k)
        rows = buf.shape[1]
        self.top, self.bottom = pl.ds(0, rows // 2), pl.ds(rows // 2, rows // 2)

    def ref(self, block, part=None):
        return self.buf.at[block] if part is None else self.buf.at[block, part]

    def go(self, slot, block, to, part=None):
        ref = self.ref(block, part)
        send(ref, ref, self.s.at[slot], self.r.at[slot], {"ctx": to})

    def got(self, slot, block, part=None):
        ref = self.ref(block, part)
        pltpu.make_async_remote_copy(
            src_ref=ref, dst_ref=ref, send_sem=self.s.at[slot], recv_sem=self.r.at[slot],
            device_id={"ctx": self.sib}, device_id_type=MESH,
        ).wait_recv()

    def sent(self, slot, block, part=None):
        ref = self.ref(block, part)
        pltpu.make_async_remote_copy(
            src_ref=ref, dst_ref=ref, send_sem=self.s.at[slot], recv_sem=self.r.at[slot],
            device_id={"ctx": self.sib}, device_id_type=MESH,
        ).wait_send()

    def start(self):
        self.go(0, self.own, self.yp, self.top)
        self.go(1, self.own, self.ym, self.bottom)
        self.go(9, self.own, self.yp, self.bottom)
        self.go(10, self.own, self.ym, self.top)
        self.go(2, self.own, self.sib)

    def middle(self):
        self.got(0, self.ym, self.top)
        self.go(5, self.ym, self.yp, self.top)
        self.got(1, self.yp, self.bottom)
        self.go(6, self.yp, self.ym, self.bottom)
        self.got(9, self.ym, self.bottom)
        self.go(3, self.ym, self.sib)
        self.got(10, self.yp, self.top)
        self.go(4, self.yp, self.sib)

    def end(self):
        self.got(5, self.y2, self.top)
        self.go(7, self.y2, self.sib, self.top)
        self.got(6, self.y2, self.bottom)
        self.go(8, self.y2, self.sib, self.bottom)

    def finish(self):
        self.got(2, self.sib)
        self.got(3, self.sym)
        self.got(4, self.syp)
        self.last()

    def last(self):
        self.got(7, self.sy2, self.top)
        self.got(8, self.sy2, self.bottom)

    def drain(self):
        self.sent(0, self.own, self.top)
        self.sent(1, self.own, self.bottom)
        self.sent(9, self.own, self.bottom)
        self.sent(10, self.own, self.top)
        self.sent(2, self.own)
        self.sent(3, self.ym)
        self.sent(4, self.yp)
        self.sent(5, self.ym, self.top)
        self.sent(6, self.yp, self.bottom)
        self.sent(7, self.y2, self.top)
        self.sent(8, self.y2, self.bottom)


ORDER = (0, 1, 7, 2, 6, 3, 5, 4)
LAG = 3


class Voc:
    def __init__(self, buf, ssem, rsem, v):
        self.buf, self.s, self.r = buf, ssem, rsem
        self.x, self.z = v // 8, v % 8
        self.v = v
        self.xp, self.xm = (self.x + 1) % 4, (self.x + 3) % 4

    def wait(self, refs, sem_s, sem_r, receive):
        copy = pltpu.make_async_remote_copy(
            src_ref=refs, dst_ref=refs, send_sem=sem_s, recv_sem=sem_r,
            device_id={"vocab": self.xp * 8 + self.z}, device_id_type=MESH,
        )
        if receive:
            copy.wait_recv()
        else:
            copy.wait_send()

    def start(self):
        for d in (1, 7, 2, 6):
            ref = self.buf.at[self.v]
            send(ref, ref, self.s.at[0], self.r.at[d], {"vocab": self.x * 8 + (self.z + d) % 8})

    def forward(self, d):
        ref = self.buf.at[self.x * 8 + (self.z + 8 - d) % 8]
        if d:
            self.wait(ref, self.s.at[0], self.r.at[d], True)
        if d in (2, 3):
            send(ref, ref, self.s.at[0], self.r.at[d + 1], {"vocab": self.x * 8 + (self.z + 1) % 8})
        if d == 6:
            send(ref, ref, self.s.at[0], self.r.at[5], {"vocab": self.x * 8 + (self.z + 7) % 8})
        send(ref, ref, self.s.at[1], self.r.at[8 + d], {"vocab": self.xp * 8 + self.z})
        send(ref, ref, self.s.at[2], self.r.at[16 + d], {"vocab": self.xm * 8 + self.z})

    def pass_on(self, d):
        zz = (self.z + 8 - d) % 8
        block = self.xm * 8 + zz
        self.wait(self.buf.at[block], self.s.at[1], self.r.at[8 + d], True)
        ref = self.buf.at[block, pl.ds(0, HALF)]
        send(ref, ref, self.s.at[3], self.r.at[24 + d], {"vocab": self.xp * 8 + self.z})
        block = self.xp * 8 + zz
        self.wait(self.buf.at[block], self.s.at[2], self.r.at[16 + d], True)
        ref = self.buf.at[block, pl.ds(HALF, HALF)]
        send(ref, ref, self.s.at[4], self.r.at[32 + d], {"vocab": self.xm * 8 + self.z})

    def spread(self, first=0, stop=8):
        for n in range(first, stop):
            self.forward(ORDER[n])
            if n >= LAG:
                self.pass_on(ORDER[n - LAG])

    def relay(self):
        for n in range(8 - LAG, 8):
            self.pass_on(ORDER[n])

    def finish(self):
        for d in ORDER:
            block = ((self.x + 2) % 4) * 8 + (self.z + 8 - d) % 8
            self.wait(self.buf.at[block, pl.ds(0, HALF)], self.s.at[3], self.r.at[24 + d], True)
            self.wait(self.buf.at[block, pl.ds(HALF, HALF)], self.s.at[4], self.r.at[32 + d], True)

    def drain(self):
        self.wait(self.buf.at[pl.ds(0, 7)], self.s.at[0], self.r.at[0], False)
        self.wait(self.buf.at[pl.ds(0, 8)], self.s.at[1], self.r.at[0], False)
        self.wait(self.buf.at[pl.ds(0, 8)], self.s.at[2], self.r.at[0], False)
        self.wait(self.buf.at[pl.ds(0, 4)], self.s.at[3], self.r.at[0], False)
        self.wait(self.buf.at[pl.ds(0, 4)], self.s.at[4], self.r.at[0], False)


class Swap:
    def __init__(self, src, dst, rel, ssem, rsem, c):
        self.src, self.dst, self.rel, self.s, self.r, self.c = src, dst, rel, ssem, rsem, c
        y, self.k = c // 2, c % 2
        self.at = lambda dy, kk: ((y + dy) % 4) * 2 + kk
        self.top, self.bottom = pl.ds(0, TOK), pl.ds(TOK, TOK)

    def copy(self, slot, arrive, src, dst, to):
        return pltpu.make_async_remote_copy(
            src_ref=src, dst_ref=dst, send_sem=self.s.at[slot], recv_sem=self.r.at[arrive],
            device_id={"ctx": to}, device_id_type=MESH,
        )

    def sends(self):
        c, k, at = self.c, self.k, self.at
        first, second = [], []
        for kk in range(2):
            first.append((5 + kk, 5 + kk, self.src.at[at(2, kk), self.top], self.rel.at[kk], at(1, k)))
            first.append((7 + kk, 7 + kk, self.src.at[at(2, kk), self.bottom], self.rel.at[2 + kk], at(3, k)))
        for kk in range(2):
            first.append((kk, k, self.src.at[at(1, kk)], self.dst.at[c], at(1, kk)))
            first.append((2 + kk, 2 + k, self.src.at[at(3, kk)], self.dst.at[c], at(3, kk)))
            second.append((9 + kk, 9 + k, self.rel.at[kk], self.dst.at[at(3, k), self.top], at(1, kk)))
            second.append((11 + kk, 11 + k, self.rel.at[2 + kk], self.dst.at[at(1, k), self.bottom], at(3, kk)))
        first.append((4, 4, self.src.at[at(0, 1 - k)], self.dst.at[c], at(0, 1 - k)))
        return first, second

    def start(self):
        for args in self.sends()[0]:
            self.copy(*args).start()

    def got(self, arrive, ref):
        self.copy(0, arrive, ref, ref, self.at(1, self.k)).wait_recv()

    def forward(self):
        for i in range(4):
            self.got(5 + i, self.rel.at[i])
        for args in self.sends()[1]:
            self.copy(*args).start()

    def finish(self):
        for kk in range(2):
            self.got(kk, self.dst.at[self.at(3, kk)])
            self.got(2 + kk, self.dst.at[self.at(1, kk)])
            self.got(9 + kk, self.dst.at[self.at(2, kk), self.top])
            self.got(11 + kk, self.dst.at[self.at(2, kk), self.bottom])
        self.got(4, self.dst.at[self.at(0, 1 - self.k)])

    def drain(self):
        first, second = self.sends()
        for args in first + second:
            self.copy(*args).wait_send()


class Many:
    def __init__(self, axis, me, peer, count, src, dst, ssem, rsem):
        self.axis, self.me, self.peer, self.count = axis, me, peer, count
        self.src, self.dst, self.ssem, self.rsem = src, dst, ssem, rsem

    def start(self, slot):
        @pl.loop(1, self.count)
        def _(d):
            to = self.peer(d)
            send(self.src(to), self.dst.at[slot], self.ssem, self.rsem, {self.axis: to})

    def whole(self):
        refs = self.dst.at[pl.ds(0, self.count - 1)]
        return pltpu.make_async_remote_copy(
            src_ref=refs, dst_ref=refs, send_sem=self.ssem, recv_sem=self.rsem,
            device_id={self.axis: self.peer(1)}, device_id_type=MESH,
        )

    def got(self):
        self.whole().wait_recv()

    def drain(self):
        self.whole().wait_send()


def kernel(*refs):
    (resid, gain, head_w, target, out_w, norm_gain, xs, gate, b_in, c_in, dt_in, decay_in, skip_in) = refs[:13]
    (gh_h, gr_h, gow_h, gx_h, gg_h, gb_o, gc_o, gdt_o, gld_o) = refs[13:22]
    (wbuf, owbuf, sbuf, nbuf, ntsend, ntbuf, logits, gall, pbuf, rel_a, rel_b, from_m, from_p, rz, gbuf,
     ubuf, vbuf, osend, obuf, es, acc, lse_b, inner_b, gsum_b, gdot_b, mean_s, mean_b, b_send, b_got, c_send, c_got, orel, nrel, xs_v, gate_v, b_v, c_v, gh_o, gr_o, gow_o, gx_o, gg_o, mcol, ycur, cbb, cb_ch0, gyb,
     lsem, ws, wr, ows, owr, gs, gr, us, ur, vs, vr, s1s, s1r, s2s, s2r, rs_s, rs_r, ms, mr, os_s, os_r, nt_s, nt_r) = refs[22:]
    c = lax.axis_index("ctx")
    v = lax.axis_index("vocab")
    x, z = v // 8, v % 8
    xp, xm, x2 = (x + 1) % 4, (x + 3) % 4, (x + 2) % 4

    lanes = pl.ds(pl.multiple_of((v // 4) * 128, 128), 128)
    barrier = pltpu.get_barrier_semaphore()

    @pl.loop(1, VOC)
    def _(d):
        pl.semaphore_signal(barrier, inc=1, device_id={"vocab": (v + d) % VOC}, device_id_type=MESH)

    @pl.loop(1, CTX)
    def _(d):
        pl.semaphore_signal(barrier, inc=1, device_id={"ctx": (c + d) % CTX}, device_id_type=MESH)

    local = [
        pltpu.make_async_copy(resid, sbuf.at[v], lsem.at[0]),
        pltpu.make_async_copy(head_w, wbuf.at[c], lsem.at[1]),
        pltpu.make_async_copy(out_w, owbuf.at[c], lsem.at[2]),
        pltpu.make_async_copy(xs, xs_v, lsem.at[3]),
        pltpu.make_async_copy(gate, gate_v, lsem.at[4]),
        pltpu.make_async_copy(b_in.at[:, lanes], b_v, lsem.at[5]),
        pltpu.make_async_copy(c_in.at[:, lanes], c_v, lsem.at[6]),
    ]
    for copy in local:
        copy.start()
    for copy in local[:2]:
        copy.wait()
    pl.semaphore_wait(barrier, VOC + CTX - 2)

    weights = Ctx(wbuf, ws, wr, c)
    outs_w = Ctx(owbuf, ows, owr, c)
    grads = Ctx(gall, gs, gr, c)
    states = Ctx(ubuf, us, ur, c)
    adjoints = Ctx(vbuf, vs, vr, c)
    stream = Voc(sbuf, s1s, s1r, v)
    back = Voc(gbuf, s2s, s2r, v)
    over_v = lambda d: (v + d) % VOC
    quarter = (v // 4) * 4
    over_g = lambda d: quarter + (v % 4 + d) % 4
    lse_x = Many("vocab", v, over_v, VOC, lambda to: lse_b.at[v], lse_b, ms.at[0], mr.at[0])
    inner_x = Many("vocab", v, over_v, VOC, lambda to: inner_b.at[v], inner_b, ms.at[1], mr.at[1])
    gsum_x = Many("vocab", v, over_g, 4, lambda to: gsum_b.at[v % 4], gsum_b, ms.at[2], mr.at[2])
    gdot_x = Many("vocab", v, over_g, 4, lambda to: gdot_b.at[v % 4], gdot_b, ms.at[3], mr.at[3])
    norms = Swap(ntsend, ntbuf, nrel, nt_s, nt_r, c)
    b_x = Many("vocab", v, over_v, VOC, lambda to: b_send.at[to], b_got, ms.at[6], mr.at[6])
    c_x = Many("vocab", v, over_v, VOC, lambda to: c_send.at[to], c_got, ms.at[5], mr.at[5])
    mean_x = Many("vocab", v, over_v, VOC, lambda to: mean_s.at[to], mean_b, ms.at[7], mr.at[7])

    puts = [
        pltpu.make_async_copy(src, dst, lsem.at[7 + n])
        for n, (src, dst) in enumerate(
            ((gh_o, gh_h), (gr_o, gr_h), (gow_o, gow_h), (gx_o, gx_h), (gg_o, gg_h))
        )
    ]
    stream.start()
    weights.start()
    stream.spread()

    for copy in local[2:]:
        copy.wait()
    b = b_v[...]
    cc = c_v[...]
    xb = xs_v[...]
    xf = xb.astype(F32)
    row_i = lax.broadcasted_iota(jnp.int32, (TOK, TOK), 0)
    col_i = lax.broadcasted_iota(jnp.int32, (TOK, TOK), 1)
    upper = (row_i <= col_i).astype(F32)
    head_of = lax.broadcasted_iota(jnp.int32, (8, TOK), 1) // 64
    sel = (head_of == lax.broadcasted_iota(jnp.int32, (8, TOK), 0)).astype(F32)
    dt = jnp.concatenate([dt_in[...], jnp.ones((4, TOK), F32)], axis=0)
    decay = jnp.concatenate([decay_in[...], jnp.zeros((4, TOK), F32)], axis=0)
    a = dot_high(decay, upper)
    last = a[:, TOK - 1 :]
    tail = jnp.exp(last - a) * dt
    a_cols = jnp.concatenate([a] * 16, axis=0).T
    cbb[...] = dot(cc, b, 1, 1)
    skip = jnp.zeros((1, TOK), F32)
    for h in range(4):
        skip = skip + sel[h : h + 1] * skip_in[h]
    low = lax.broadcasted_iota(jnp.int32, (TOK, 128), 1) < 64
    for pair in range(2):
        outs = []
        for h in (2 * pair, 2 * pair + 1):
            gap = a_cols[:, h : h + 1] - a[h : h + 1]
            e = jnp.exp(jnp.where(row_i >= col_i, gap, -1e30)) * dt[h : h + 1]
            es[h] = e
            outs.append(dot_left(cbb[...] * e, xb[:, pair * 128 : pair * 128 + 128]))
        ycur[:, pair * 128 : pair * 128 + 128] = jnp.where(low, outs[0], outs[1])
    tail_full = dot_high(tail, sel, 0, 0)
    grow_full = dot_high(jnp.exp(a), sel, 0, 0)
    ubuf[c, 0:128] = dot_right(b, tail_full * xf, 0, 0)
    whole = dot_high(jnp.broadcast_to(jnp.exp(last), (8, 128)), sel, 0, 0)
    ubuf[c, 128:STATE_ROWS] = whole[0 : STATE_ROWS - 128]

    stream.relay()
    weights.middle()
    stream.finish()

    def square(i, total):
        block = sbuf[i].astype(F32)
        return total + block * block

    total = lax.fori_loop(0, VOC, square, jnp.zeros((TOK, 128), F32))
    inv = lax.rsqrt(jnp.sum(total, axis=1, keepdims=True) * (1.0 / D) + EPS)
    inv = jnp.broadcast_to(inv, (TOK, 128))

    @pl.loop(0, CTX)
    def _(i):
        parts = []
        for j in range(4):
            parts.append((sbuf[4 * i + j].astype(F32) * inv * gain[4 * i + j]).astype(BF16))
        block = jnp.concatenate(parts, axis=1)
        nbuf[i] = block
        ntsend[i] = block.T

    ntbuf[c] = ntsend[c]

    def logit(i, first=False):
        part = dot(nbuf[i], wbuf[i])
        if first:
            logits[...] = part
        else:
            logits[...] += part

    logit(weights.own, True)
    weights.got(2, weights.sib)
    logit(weights.sib)
    logit(weights.ym)
    logit(weights.yp)
    weights.end()
    logit(weights.y2)
    weights.got(3, weights.sym)
    logit(weights.sym)
    weights.got(4, weights.syp)
    logit(weights.syp)
    weights.last()
    logit(weights.sy2)

    states.start()
    outs_w.start()

    @pl.loop(0, 4)
    def _(i):
        rows = pl.ds(pl.multiple_of(i * 64, 64), 64)
        part = logits[rows, :]
        most = jnp.max(part, axis=1, keepdims=True)
        value = most + jnp.log(jnp.sum(jnp.exp(part - most), axis=1, keepdims=True))
        mcol[rows, :] = jnp.broadcast_to(value, (64, 128))

    lse_b[v] = row_of(mcol[...])
    lse_x.start(v)
    target_col = column(target[...].astype(F32))
    lse_x.got()
    every = lse_b[...]
    most = jnp.max(every, axis=0)
    log_norm = most + jnp.log(jnp.sum(jnp.exp(every - most[None]), axis=0))
    mcol[...] = column(log_norm)
    cb_ch0[:, 0:128] = target_col

    base = (v * 1024).astype(F32)
    ids = lax.broadcasted_iota(jnp.int32, (64, 1024), 1).astype(F32) + base

    @pl.loop(0, 4)
    def _(i):
        rows = pl.ds(pl.multiple_of(i * 64, 64), 64)
        part = logits[rows, :]
        hit = jnp.where(wide(cb_ch0[rows, 0:128], 1024) == ids, 1.0, 0.0)
        g = (jnp.exp(part - wide(mcol[rows, :], 1024)) - hit).astype(BF16)
        gall[c, rows, :] = g
        value = jnp.sum(g.astype(F32) * part, axis=1, keepdims=True)
        mcol[rows, :] = jnp.broadcast_to(value, (64, 128))
        value = jnp.sum(g.astype(F32), axis=1, keepdims=True)
        cb_ch0[rows, 128:256] = jnp.broadcast_to(value, (64, 128))

    inner_b[v, 0:1] = row_of(mcol[...])
    inner_b[v, 1:2] = row_of(cb_ch0[:, 128:256])
    inner_x.start(v)

    top, bottom = pl.ds(0, HALF), pl.ds(HALF, HALF)

    weigh = jnp.concatenate([gall[c], jnp.full((16, 1024), 2.0**-10, BF16)], axis=0)
    sums_g = cb_ch0[:, 128:256]

    def partial(i):
        part = dot(weigh, wbuf[i], 1, 1)
        for j in range(4):
            mean = part[TOK : TOK + 1, j * 128 : j * 128 + 128]
            mean_s[4 * i + j] = mean
            pbuf[4 * i + j] = (part[0:TOK, j * 128 : j * 128 + 128] - sums_g * mean).astype(BF16)

    to_p, to_m = {"vocab": xp * 8 + z}, {"vocab": xm * 8 + z}

    def rs_send(kind, n, src, dst, to):
        send(src, dst, rs_s.at[kind], rs_r.at[8 * kind + n], to)

    def rs_wait(kind, n, ref, receive=True):
        copy = pltpu.make_async_remote_copy(
            src_ref=ref, dst_ref=ref, send_sem=rs_s.at[kind], recv_sem=rs_r.at[8 * kind + n],
            device_id=to_p, device_id_type=MESH,
        )
        if receive:
            copy.wait_recv()
        else:
            copy.wait_send()

    far, near = 1 - z // 4, z // 4
    serve = [4 * far + (z % 4 + 1 + j) % 4 for j in range(4)] + [4 * near + (z % 4 + 1 + j) % 4 for j in range(4)]
    def first_relays(ns):
        for n in ns:
            rs_send(0, n, pbuf.at[x2 * 8 + serve[n], top], rel_a.at[n], to_p)
            rs_send(1, n, pbuf.at[x2 * 8 + serve[n], bottom], rel_b.at[n], to_m)

    def relayed(n):
        rs_wait(0, n, rel_a.at[n])
        i = xp * 8 + serve[n]
        pbuf[i, 0:HALF] = (pbuf[i, 0:HALF].astype(F32) + rel_a[n].astype(F32)).astype(BF16)
        rs_send(2, n, pbuf.at[i], from_m.at[n], to_p)
        rs_wait(1, n, rel_b.at[n])
        i = xm * 8 + serve[n]
        pbuf[i, HALF:TOK] = (pbuf[i, HALF:TOK].astype(F32) + rel_b[n].astype(F32)).astype(BF16)
        rs_send(3, n, pbuf.at[i], from_p.at[n], to_m)

    def collect(n):
        rs_wait(2, n, from_m.at[n])
        rs_wait(3, n, from_p.at[n])
        i = x * 8 + serve[n]
        total = pbuf[i].astype(F32) + from_m[n].astype(F32) + from_p[n].astype(F32)
        pbuf[i] = total.astype(BF16)
        if n < 7:
            send(pbuf.at[i], rz.at[z], rs_s.at[4], rs_r.at[32], {"vocab": i})

    partial(2 * x2 + far)
    first_relays(range(4))
    partial(2 * xp + far)
    partial(2 * xm + far)
    for n in range(4):
        relayed(n)
    partial(2 * x2 + near)
    first_relays(range(4, 8))
    grads.start()
    partial(2 * x + far)
    partial(2 * xp + near)
    partial(2 * xm + near)
    partial(2 * x + near)
    mean_b[v] = mean_s[v]
    mean_x.start(v)
    states.middle()
    outs_w.middle()
    norms.start()

    for n in range(4):
        collect(n)
    for n in range(4, 8):
        relayed(n)
    for n in range(4, 8):
        collect(n)
    rz[z] = pbuf[v]

    inner_x.got()
    inner = column(jnp.sum(inner_b[...], axis=0)[0:1])
    mean_x.got()
    extra = dot_high(inner_b[:, 1, :], mean_b[:, 0, :], 0, 0)
    resid_f = sbuf[v].astype(F32)
    less = resid_f * (inv * inv * inner * (1.0 / D))
    rs_wait(4, 0, rz.at[pl.ds(0, 7)])
    total = extra
    for j in range(8):
        total = total + rz[j].astype(F32)
    mine = (inv * (total * gain[v]) - less).astype(BF16)
    gr_o[...] = mine
    puts[1].start()
    gbuf[v] = mine
    back.start()
    back.spread(0, 5)
    states.end()
    outs_w.end()
    back.spread(5, 8)
    norms.forward()
    back.relay()
    states.finish()

    def enter(j, h0):
        new = ubuf[j, 128:129] * h0 + ubuf[j, 0:128]
        return jnp.where(j < c, new, h0)

    h0 = lax.fori_loop(0, CTX - 1, enter, jnp.zeros((128, TOK), F32))
    vbuf[c, 0:128] = h0
    ch0 = dot_right(cc, h0) * grow_full
    cb_ch0[...] = ch0
    y = ycur[...] + ch0 + skip * xf
    ycur[...] = y
    zf = gate_v[...].astype(F32)
    sig = 1.0 / (1.0 + jnp.exp(-zf))
    gated = y * zf * sig
    squares = dot_high(jnp.ones((8, TOK), F32), gated * gated, 1, 1)
    gsum_b[v % 4] = squares[0:1]
    gsum_x.start(v % 4)

    ng = norm_gain[...]
    outs_w.finish()

    def project(t, total):
        i = (2 * x2 + 2 + t) % CTX
        lhs = jnp.concatenate([gbuf[4 * i + j] for j in range(4)], axis=1)
        return total + dot(lhs, owbuf[i], 1, 1)

    grad_normed = lax.fori_loop(0, 6, project, jnp.zeros((TOK, TOK), F32))
    grads.middle()
    back.finish()
    grad_normed = lax.fori_loop(6, CTX, project, grad_normed)
    scaled = grad_normed * ng
    dots = dot_high(jnp.ones((8, TOK), F32), gated * scaled, 1, 1)
    gdot_b[v % 4] = dots[0:1]
    gdot_x.start(v % 4)
    gsum_x.got()
    sums = jnp.sum(gsum_b[...], axis=0)
    ginv = column(lax.rsqrt(sums * (1.0 / (INNER // GROUPS)) + EPS))
    ginv = wide(ginv, TOK)
    normed_t = (gated * ginv * ng).astype(BF16).T

    @pl.loop(0, CTX)
    def _(i):
        lhs = jnp.concatenate([gbuf[4 * i + j] for j in range(4)], axis=1)
        osend[(i % 2) * 4 + i // 2] = dot(normed_t, lhs).astype(BF16)

    y_at, k_at = c // 2, c % 2
    side, c_p, c_m = y_at * 2 + 1 - k_at, ((y_at + 1) % 4) * 2 + k_at, ((y_at + 3) % 4) * 2 + k_at
    at_p, at_m, at_2 = k_at * 4 + (y_at + 1) % 4, k_at * 4 + (y_at + 3) % 4, k_at * 4 + (y_at + 2) % 4

    def os_copy(n, src, dst, to):
        return pltpu.make_async_remote_copy(
            src_ref=src, dst_ref=dst, send_sem=os_s.at[n], recv_sem=os_r.at[n], device_id={"ctx": to}, device_id_type=MESH
        )

    os_copies = (
        os_copy(0, osend.at[pl.ds((1 - k_at) * 4, 4)], obuf.at[pl.ds(0, 4)], side),
        os_copy(1, osend.at[at_2, top], orel.at[0], c_p),
        os_copy(2, osend.at[at_2, bottom], orel.at[1], c_m),
        os_copy(3, osend.at[at_p], obuf.at[4], c_p),
        os_copy(4, osend.at[at_m], obuf.at[5], c_m),
    )
    os_copies[0].start()
    gdot_x.got()
    gdot = wide(column(jnp.sum(gdot_b[...], axis=0)), TOK)
    grad_gated = ginv * scaled - gated * (ginv * ginv * ginv * gdot * (1.0 / (INNER // GROUPS)))
    gg_o[...] = (grad_gated * y * sig * (1.0 + zf * (1.0 - sig))).astype(BF16)
    gy = grad_gated * zf * sig
    gyb[...] = gy
    puts[4].start()
    gye = gy * grow_full
    h0 = vbuf[c, 0:128]
    dc = dot_both(gye, h0, 1, 1)
    vbuf[c, 0:128] = dot_right(cc, gye, 0, 0)
    adjoints.start()

    ones8 = jnp.ones((8, TOK), F32)
    dcb = jnp.zeros((TOK, TOK), F32)
    rows_m, cols_m = [], []
    for h in range(4):
        if h == 2:
            os_copies[0].wait_recv()
            for j in range(1, 4):
                i = k_at * 4 + (y_at + 4 - j) % 4
                osend[i] = (osend[i].astype(F32) + obuf[(y_at + 4 - j) % 4].astype(F32)).astype(BF16)
        pair = h // 2
        gyp = gyb[:, pair * 128 : pair * 128 + 128]
        gym = jnp.where(low if h % 2 == 0 else jnp.logical_not(low), gyp, 0.0)
        e = es[h]
        s = cbb[...] * e
        ds = dot_left(gym, xb[:, pair * 128 : pair * 128 + 128], 1, 1)
        dcb = dcb + ds * e
        m = ds * s
        rows_m.append(dot_high(ones8, m, 1, 1)[0:1])
        cols_m.append(jnp.sum(m, axis=0, keepdims=True))
        part = dot_both(s, gym, 0, 0)
        if h % 2 == 0:
            held = part
        else:
            logits[:, pair * 128 : pair * 128 + 128] = held + part
    adjoints.middle()
    os_copies[1].start()
    os_copies[2].start()
    zero4 = jnp.zeros((4, TOK), F32)
    rows_m = jnp.concatenate(rows_m + [zero4], axis=0)
    cols_m = jnp.concatenate(cols_m + [zero4], axis=0)
    dc = dc + dot_left(dcb, b)
    db = dot_left(dcb, cc, 0, 0)
    r_rows = dot_high(sel, gy * cb_ch0[...], 1, 1)
    c_send[...] = dc.reshape(VOC, 8, 128).astype(BF16)
    c_x.start(v)
    c_got[v] = c_send[v]
    adjoints.end()
    os_copies[1].wait_recv()
    osend[at_p, top] = (osend[at_p, top].astype(F32) + orel[0].astype(F32)).astype(BF16)
    os_copies[3].start()
    os_copies[2].wait_recv()
    osend[at_m, bottom] = (osend[at_m, bottom].astype(F32) + orel[1].astype(F32)).astype(BF16)
    os_copies[4].start()
    adjoints.finish()
    grads.end()

    def leave(j, h1):
        i = CTX - 1 - j
        new = ubuf[i, 128:129] * h1 + vbuf[i, 0:128]
        return jnp.where(i > c, new, h1)

    h1 = lax.fori_loop(0, CTX - 1, leave, jnp.zeros((128, TOK), F32))
    db = db + dot_both(tail_full * xf, h1, 1, 1)
    b_send[...] = db.reshape(VOC, 8, 128).astype(BF16)
    b_x.start(v)
    b_got[v] = b_send[v]
    bdh = dot_right(b, h1) * tail_full
    gx_o[...] = (logits[:, 0:TOK] + skip * gy + bdh).astype(BF16)
    puts[3].start()
    wq = dot_high(sel, bdh * xf, 1, 1)

    def again(j, h0):
        new = ubuf[j, 128:129] * h0 + ubuf[j, 0:128]
        return jnp.where(j < c, new, h0)

    h0 = lax.fori_loop(0, CTX - 1, again, jnp.zeros((128, TOK), F32))
    cross = jnp.sum(h0 * h1, axis=0, keepdims=True) * ubuf[c, 128:129]
    cross = dot_high(sel, jnp.broadcast_to(cross, (8, TOK)), 1, 1)[:, 0:1]
    gdt_o[...] = ((cols_m + wq) / dt)[0:4]
    da = rows_m - cols_m + r_rows - wq
    at_end = cross + jnp.sum(wq, axis=1, keepdims=True)
    gld_o[...] = (dot_high(da, (row_i >= col_i).astype(F32)) + at_end)[0:4]

    grads.finish()
    norms.finish()
    acc[...] = jnp.zeros_like(acc)

    @pl.loop(0, CTX)
    def _(i):
        acc[...] += dot(ntbuf[i], gall[i])

    gh_o[...] = acc[...].astype(BF16)
    puts[0].start()

    os_copies[3].wait_recv()
    os_copies[4].wait_recv()
    mine = k_at * 4 + y_at
    for j in range(4):
        cols = pl.ds(128 * j, 128)
        total = osend[mine, :, cols].astype(F32) + obuf[y_at, :, cols].astype(F32)
        gow_o[:, cols] = (total + obuf[4, :, cols].astype(F32) + obuf[5, :, cols].astype(F32)).astype(BF16)
    puts[2].start()
    c_x.got()
    b_x.got()
    for got, out in ((b_got, gb_o), (c_got, gc_o)):
        parts = []
        for g in range(GROUPS):
            four = [got[4 * g + j].astype(F32) for j in range(4)]
            parts.append((four[0] + four[1]) + (four[2] + four[3]))
        out[...] = jnp.concatenate(parts, axis=1).astype(BF16)

    for gather in (weights, outs_w, grads, states, adjoints):
        gather.drain()
    norms.drain()
    stream.drain()
    back.drain()
    for many in (lse_x, inner_x, gsum_x, gdot_x, b_x, c_x, mean_x):
        many.drain()
    rs_wait(0, 0, rel_a, False)
    rs_wait(1, 0, rel_b, False)
    rs_wait(2, 0, from_m, False)
    rs_wait(3, 0, from_p, False)
    rs_wait(4, 0, rz.at[pl.ds(0, 7)], False)
    for copy in os_copies:
        copy.wait_send()
    for copy in puts:
        copy.wait()


def copy_kernel(*refs):
    n = (len(refs) - 2) // 3
    ins, outs, bufs, (sin, sout) = refs[:n], refs[n : 2 * n], refs[2 * n : 3 * n], refs[3 * n :]
    parts = []
    for i in range(n):
        rows = ins[i].shape[0]
        step = rows // 4 if rows >= 512 else rows
        parts += [(i, pl.ds(r, step)) for r in range(0, rows, step)]
    loads = [pltpu.make_async_copy(ins[i].at[r], bufs[i].at[r], sin.at[m]) for m, (i, r) in enumerate(parts)]
    stores = [pltpu.make_async_copy(bufs[i].at[r], outs[i].at[r], sout.at[m]) for m, (i, r) in enumerate(parts)]
    for copy in loads:
        copy.start()
    for load, store in zip(loads, stores):
        load.wait()
        store.start()
    for store in stores:
        store.wait()


def hand_over(arrays):
    n = len(arrays)
    hbm = pl.BlockSpec(memory_space=pl.ANY)
    return pl.pallas_call(
        copy_kernel,
        out_shape=tuple(jax.ShapeDtypeStruct(a.shape, a.dtype) for a in arrays),
        in_specs=[hbm] * n,
        out_specs=(hbm,) * n,
        scratch_shapes=[pltpu.VMEM(a.shape, a.dtype) for a in arrays]
        + [pltpu.SemaphoreType.DMA((n + 3,)), pltpu.SemaphoreType.DMA((n + 3,))],
        name="hand_over",
    )(*arrays)


def shards(resid, gain, head_w, targets, out_w, norm_gain, xs, gate, b, c, dt, decay, skip):
    heads = skip.shape[0]
    args = (
        resid,
        gain.reshape(VOC, 1, 128),
        head_w,
        targets.reshape(1, TOK),
        out_w,
        norm_gain.reshape(1, TOK),
        xs,
        gate,
        b,
        c,
        dt,
        decay,
        skip,
    )
    vm = pl.BlockSpec(memory_space=pltpu.VMEM)
    hbm = pl.BlockSpec(memory_space=pl.ANY)
    shape = jax.ShapeDtypeStruct
    dma = pltpu.SemaphoreType.DMA
    scratch = [
        pltpu.VMEM((CTX, 512, 1024), BF16),
        pltpu.VMEM((CTX, TOK, 512), BF16),
        pltpu.VMEM((VOC, TOK, 128), BF16),
        pltpu.VMEM((CTX, TOK, 512), BF16),
        pltpu.VMEM((CTX, 512, TOK), BF16),
        pltpu.VMEM((CTX, 512, TOK), BF16),
        pltpu.VMEM((TOK, 1024), F32),
        pltpu.VMEM((CTX, TOK, 1024), BF16),
        pltpu.VMEM((VOC, TOK, 128), BF16),
        pltpu.VMEM((8, HALF, 128), BF16),
        pltpu.VMEM((8, HALF, 128), BF16),
        pltpu.VMEM((8, TOK, 128), BF16),
        pltpu.VMEM((8, TOK, 128), BF16),
        pltpu.VMEM((8, TOK, 128), BF16),
        pltpu.VMEM((VOC, TOK, 128), BF16),
        pltpu.VMEM((CTX, STATE_ROWS, TOK), F32),
        pltpu.VMEM((CTX, 128, TOK), F32),
        pltpu.VMEM((CTX, TOK, 512), BF16),
        pltpu.VMEM((CTX, TOK, 512), BF16),
        pltpu.VMEM((4, TOK, TOK), F32),
        pltpu.VMEM((512, 1024), F32),
        pltpu.VMEM((VOC, 1, TOK), F32),
        pltpu.VMEM((VOC, 2, TOK), F32),
        pltpu.VMEM((4, 1, TOK), F32),
        pltpu.VMEM((4, 1, TOK), F32),
        pltpu.VMEM((VOC, 1, 128), F32),
        pltpu.VMEM((VOC, 1, 128), F32),
        pltpu.VMEM((VOC, 8, 128), BF16),
        pltpu.VMEM((VOC, 8, 128), BF16),
        pltpu.VMEM((VOC, 8, 128), BF16),
        pltpu.VMEM((VOC, 8, 128), BF16),
        pltpu.VMEM((2, HALF, 512), BF16),
        pltpu.VMEM((4, TOK, TOK), BF16),
        pltpu.VMEM((TOK, TOK), BF16),
        pltpu.VMEM((TOK, TOK), BF16),
        pltpu.VMEM((TOK, 128), BF16),
        pltpu.VMEM((TOK, 128), BF16),
        pltpu.VMEM((512, 1024), BF16),
        pltpu.VMEM((TOK, 128), BF16),
        pltpu.VMEM((TOK, 512), BF16),
        pltpu.VMEM((TOK, TOK), BF16),
        pltpu.VMEM((TOK, TOK), BF16),
        pltpu.VMEM((TOK, 128), F32),
        pltpu.VMEM((TOK, TOK), F32),
        pltpu.VMEM((TOK, TOK), F32),
        pltpu.VMEM((TOK, TOK), F32),
        pltpu.VMEM((TOK, TOK), F32),
        dma((12,)),
        dma((11,)), dma((11,)), dma((11,)), dma((11,)), dma((11,)), dma((11,)), dma((11,)), dma((11,)), dma((11,)), dma((11,)),
        dma((5,)), dma((40,)), dma((5,)), dma((40,)),
        dma((5,)), dma((33,)),
        dma((8,)), dma((8,)),
        dma((5,)), dma((5,)),
        dma((13,)), dma((13,)),
    ]
    outs = pl.pallas_call(
        kernel,
        out_shape=(
            shape((512, 1024), BF16),
            shape((TOK, 128), BF16),
            shape((TOK, 512), BF16),
            shape((TOK, TOK), BF16),
            shape((TOK, TOK), BF16),
            shape((8, 1024), BF16),
            shape((8, 1024), BF16),
            shape((heads, TOK), F32),
            shape((heads, TOK), F32),
        ),
        in_specs=[hbm, vm, hbm, vm, hbm, vm, hbm, hbm, hbm, hbm, vm, vm] + [pl.BlockSpec(memory_space=pltpu.SMEM)],
        out_specs=(hbm,) * 5 + (vm,) * 4,
        scratch_shapes=scratch,
        compiler_params=pltpu.CompilerParams(
            collective_id=0, has_side_effects=True, vmem_limit_bytes=67043328
        ),
        name="step",
    )(*args)
    return hand_over(outs)


def solution(mesh):
    return jax.shard_map(
        shards,
        mesh=mesh,
        in_specs=(
            P("ctx", "vocab"),
            P(),
            P("ctx", "vocab"),
            P("ctx"),
            P("vocab", "ctx"),
            P("vocab"),
            P("ctx", "vocab"),
            P("ctx", "vocab"),
            P("ctx", None),
            P("ctx", None),
            P("vocab", "ctx"),
            P("vocab", "ctx"),
            P("vocab"),
        ),
        out_specs=(
            P("ctx", "vocab"),
            P("ctx", "vocab"),
            P("vocab", "ctx"),
            P("ctx", "vocab"),
            P("ctx", "vocab"),
            P(("ctx", "vocab"), None),
            P(("ctx", "vocab"), None),
            P("vocab", "ctx"),
            P("vocab", "ctx"),
        ),
        check_vma=False,
    )
```
